256 devices in a mesh: strip: 4 (over x), lvl: 64 (over z, y, core).
Axes of the slice: x: 4, y: 4, z: 8, core: 2. Of those that a mesh axis runs over, the one named last changes fastest.
Arguments:
- photos: bfloat16 [16, 3, 64, 65536], P('strip', None, None, 'lvl'), may hold values from -6 to 6
- seams: int32 [16, 2, 64], P('strip'), may hold values from 0 to 65536, as said below
- offsets: int32 [16], P('strip'), may hold values from 0 to 2, as said below
Outputs:
- blended: float32 [3, 128, 65536], P(None, 'strip', 'lvl')
The draws below stay inside these ranges and needn't reach their ends.
Inputs may be any that keep to these rules, and one draw needn't show every extreme that they name: offsets[p] differs from p // 4 by at most 2; every strip is the first or the second strip of some photo. seams[p, 0, r] <= seams[p, 1, r]; in each panorama row the intervals of the photos that cover it are disjoint and together cover all 65536 columns.
All inputs are finite; a program needn't handle non-finite values.
Results may differ from the reference program's by a relative error of at most 0.003.
Values may be sent and summed in bfloat16 or wider, within the bound.
A program may use at most 64 MiB of HBM per device.

```python
import jax
import jax.numpy as jnp
from jax import lax

CH = 3
LEVELS = 6
SPREAD = 2
P_DEV = 4
R_DEV = 32
PHOTOS = 16
NC = 65536
N_STRIP = 4


def layout(key):
    strips = PHOTOS // P_DEV
    inner = jax.random.fold_in(key, 7)
    first_key, second_key = jax.random.split(inner, 2)
    owner = jnp.arange(PHOTOS, dtype=jnp.int32) // P_DEV
    slot = jnp.arange(PHOTOS, dtype=jnp.int32) % P_DEV
    jitter = jax.random.randint(first_key, (PHOTOS,), -SPREAD, SPREAD + 1, dtype=jnp.int32)
    shift_by = jnp.where(slot == 0, -SPREAD, jnp.where(slot == 1, SPREAD, jnp.where(slot == 2, 0, jitter)))
    offsets = jnp.clip(owner + shift_by, 0, strips - 2).astype(jnp.int32)
    rows = jnp.arange(PHOTOS // P_DEV * R_DEV, dtype=jnp.int32)
    relative = rows[None, :] // R_DEV - offsets[:, None]
    cover = ((relative == 0) | (relative == 1)).astype(jnp.int32)
    shares = jax.random.randint(second_key, cover.shape, 1, 65, dtype=jnp.int32) * cover
    running = jnp.cumsum(shares, axis=0, dtype=jnp.int32)
    total = running[-1:]
    before = running - shares
    left_edge = NC * before // total
    right_edge = NC * running // total
    local = offsets[:, None] * R_DEV + jnp.arange(2 * R_DEV, dtype=jnp.int32)[None, :]
    left_rows = jnp.take_along_axis(left_edge, local, axis=1)
    right_rows = jnp.take_along_axis(right_edge, local, axis=1)
    seams = jnp.stack([left_rows, right_rows], axis=1).astype(jnp.int32)
    return (offsets, seams)


def draw_offsets(key, part):
    return layout(key)[0]


def draw_seams(key, part):
    return layout(key)[1]


def draw_photos(key, part):
    inner = jax.random.fold_in(key, 11)
    noise_key, level_key, phase_key, cycle_key = jax.random.split(inner, 4)
    shape = (PHOTOS, CH, 2 * R_DEV, NC)
    column = jnp.arange(NC, dtype=jnp.float32)[None, None, None, :] / NC
    phase = jax.random.uniform(phase_key, (PHOTOS, CH, 1, 1), jnp.float32, 0.0, 6.2831853)
    cycles = jax.random.uniform(cycle_key, (PHOTOS, CH, 1, 1), jnp.float32, 1.0, 4.0)
    ramp = jnp.sin(6.2831853 * cycles * column + phase)
    rough = jax.random.normal(noise_key, shape, jnp.float32)
    level = jax.random.uniform(level_key, (PHOTOS, CH, 1, 1), jnp.float32, -3.0, 3.0)
    smooth = level + 1.5 * ramp
    return jnp.clip(rough + smooth, -6.0, 6.0).astype(jnp.bfloat16)


def setup_inputs(seed: int = 0) -> dict:
    streams_of = jax.random.split(jax.random.key(seed), 4)
    return {
        "photos": draw_photos(jax.random.fold_in(streams_of[3], 71), 0),
        "seams": draw_seams(jax.random.fold_in(streams_of[3], 71), 0),
        "offsets": draw_offsets(jax.random.fold_in(streams_of[3], 71), 0),
    }


TAPS = (0.0625, 0.25, 0.375, 0.25, 0.0625)


def reduce_padded(padded):
    rows = padded.shape[-2] - 4
    cols = padded.shape[-1] - 4
    vertical = TAPS[0] * padded[..., 0:rows:2, :]
    for tap in range(1, 5):
        vertical = vertical + TAPS[tap] * padded[..., tap:tap + rows:2, :]
    result = TAPS[0] * vertical[..., 0:cols:2]
    for tap in range(1, 5):
        result = result + TAPS[tap] * vertical[..., tap:tap + cols:2]
    return result


def expand_padded(padded):
    even = (padded[..., :-2, :] + 6.0 * padded[..., 1:-1, :] + padded[..., 2:, :]) * 0.125
    odd = (padded[..., 1:-1, :] + padded[..., 2:, :]) * 0.5
    both = jnp.stack([even, odd], axis=-2)
    tall = both.reshape(both.shape[:-3] + (2 * both.shape[-3], both.shape[-1]))
    even = (tall[..., :-2] + 6.0 * tall[..., 1:-1] + tall[..., 2:]) * 0.125
    odd = (tall[..., 1:-1] + tall[..., 2:]) * 0.5
    both = jnp.stack([even, odd], axis=-1)
    return both.reshape(both.shape[:-2] + (2 * both.shape[-2],))


def pad_all(field, width):
    return jnp.pad(field, [(0, 0)] * (field.ndim - 2) + [(width, width), (width, width)])


def photo_levels(image, seam, column):
    mask = ((column[None, :] >= seam[0][:, None]) & (column[None, :] < seam[1][:, None])).astype(jnp.float32)
    level = jnp.concatenate([image.astype(jnp.float32), mask[None]], axis=0)
    gauss = [level]
    for step in range(LEVELS - 1):
        gauss.append(reduce_padded(pad_all(gauss[-1], 2)))
    weighted = []
    for step in range(LEVELS):
        detail = gauss[step][:CH]
        if step + 1 < LEVELS:
            detail = detail - expand_padded(pad_all(gauss[step + 1][:CH], 1))
        weighted.append((gauss[step][CH:] * detail).astype(jnp.bfloat16))
    return weighted


def reference(photos, seams, offsets):
    column = jnp.arange(NC, dtype=jnp.int32)
    span = 2 * SPREAD + 2
    canvases = tuple(jnp.zeros((CH, (N_STRIP + span - 1) * (R_DEV >> step), NC >> step), jnp.float32) for step in range(LEVELS))

    def owner_step(owner, canvases):
        windows = [jnp.zeros((CH, span * (R_DEV >> step), NC >> step), jnp.float32) for step in range(LEVELS)]
        for slot in range(P_DEV):
            index = (owner * P_DEV + slot).astype(jnp.int32)
            image = lax.dynamic_index_in_dim(photos, index, 0, keepdims=False)
            seam = lax.dynamic_index_in_dim(seams, index, 0, keepdims=False)
            place = lax.dynamic_index_in_dim(offsets, index, 0, keepdims=False)
            levels = photo_levels(image, seam, column)
            for step in range(LEVELS):
                start = ((place - owner + SPREAD) * (R_DEV >> step)).astype(jnp.int32)
                zero = jnp.zeros((), jnp.int32)
                current = lax.dynamic_slice(windows[step], (zero, start, zero), levels[step].shape)
                windows[step] = lax.dynamic_update_slice(windows[step], current + levels[step].astype(jnp.float32), (zero, start, zero))
        updated = []
        for step in range(LEVELS):
            rounded = windows[step].astype(jnp.bfloat16).astype(jnp.float32)
            start = (owner * (R_DEV >> step)).astype(jnp.int32)
            zero = jnp.zeros((), jnp.int32)
            current = lax.dynamic_slice(canvases[step], (zero, start, zero), rounded.shape)
            updated.append(lax.dynamic_update_slice(canvases[step], current + rounded, (zero, start, zero)))
        return tuple(updated)

    canvases = lax.fori_loop(0, N_STRIP, owner_step, canvases)
    bands = [canvases[step][:, SPREAD * (R_DEV >> step):(SPREAD + N_STRIP) * (R_DEV >> step)] for step in range(LEVELS)]
    total = bands[LEVELS - 1]
    for step in range(LEVELS - 2, -1, -1):
        total = bands[step] + expand_padded(pad_all(total, 1))
    return total
```

```python
import functools

import jax
import jax.numpy as jnp
import ml_dtypes
import numpy as np
from jax import lax
from jax.experimental import pallas as pl
from jax.experimental.pallas import tpu as pltpu
from jax.sharding import PartitionSpec as P

BF = jnp.bfloat16
F32 = jnp.float32
MESH = pl.DeviceIdType.MESH
TAPS = (0.0625, 0.25, 0.375, 0.25, 0.0625)
N = 1024
HALO = 128
WIDE = {0: 1280, 1: 640, 2: 320, 3: 160, 4: 80, 5: 40}
PAD = {1: 640, 2: 384, 3: 256, 4: 128, 5: 128}
ROWS = {0: 64, 1: 32, 2: 16, 3: 8, 4: 4, 5: 2}
SLOT = {2: (0, 64), 3: (64, 32), 4: (96, 16), 5: (112, 16)}


def reduce_rows(tall):
    m = np.zeros((tall // 2, tall))
    for i in range(tall // 2):
        for t in range(5):
            r = 2 * i + t - 2
            if 0 <= r < tall:
                m[i, r] = TAPS[t]
    return m


def expand_rows(tall):
    m = np.zeros((2 * tall, tall))
    for i in range(tall):
        for r, w in ((i - 1, 0.125), (i, 0.75), (i + 1, 0.125)):
            if 0 <= r < tall:
                m[2 * i, r] = w
        for r in (i, i + 1):
            if r < tall:
                m[2 * i + 1, r] = 0.5
    return m


def blocks(m, count):
    return np.kron(np.eye(count), m)


def bf(x):
    return np.asarray(x, np.float32).astype(ml_dtypes.bfloat16)


def split(x):
    hi = bf(x)
    return hi, bf(np.asarray(x, np.float64) - hi.astype(np.float64))


def valid(level, edge):
    e = np.arange(WIDE[level])
    h = HALO >> level
    n = N >> level
    keep = np.ones(WIDE[level])
    if edge == 0:
        keep[e < h] = 0
    if edge == 2:
        keep[e >= h + n] = 0
    return keep


def reduce_cols(level, edge):
    m = reduce_rows(WIDE[level]).T
    return m * valid(level + 1, edge)[None, :]


def constants():
    c = {}
    c["v1"] = bf(blocks(reduce_rows(64), 4))
    w = np.zeros((512, 128))
    for col in range(128):
        for t in range(5):
            w[128 + 2 * col + t - 2, col] = TAPS[t]
    c["wred"] = bf(w)
    v = {1: np.eye(32)}
    for k in (2, 3, 4, 5):
        v[k] = reduce_rows(ROWS[k - 1]) @ v[k - 1]
    v25 = np.zeros((128, 128))
    for k in (2, 3, 4, 5):
        start, _ = SLOT[k]
        v25[start : start + 4 * ROWS[k]] = blocks(v[k], 4)
    c["v25"] = bf(v25)
    h35 = np.zeros((3, 384, 384))
    for edge in range(3):
        m3 = reduce_cols(2, edge)
        m4 = m3 @ reduce_cols(3, edge)
        m5 = m4 @ reduce_cols(4, edge)
        h35[edge, :320, 0:160] = m3
        h35[edge, :320, 256:336] = m4
        h35[edge, :320, 336:376] = m5
    c["h35"] = bf(h35)
    c["er1"] = bf(blocks(expand_rows(16), 12))
    c["er2"] = bf(blocks(expand_rows(8), 12))
    c["er3"] = bf(blocks(expand_rows(4), 12))
    er4 = np.zeros((48, 48))
    for ch in range(3):
        er4[16 * ch : 16 * ch + 16, 16 * ch : 16 * ch + 8] = blocks(expand_rows(2), 4)
    c["er4"] = bf(er4)
    for k in (1, 2, 3, 4):
        m = np.zeros((PAD[k + 1], PAD[k]))
        at = 80 if k == 4 else 0
        m[at : at + WIDE[k + 1], : WIDE[k]] = expand_rows(WIDE[k + 1]).T
        c[f"ec{k}"] = bf(m)
    e0 = np.zeros((256, 256))
    for col in range(256):
        i = 64 + col // 2
        if col % 2 == 0:
            e0[i - 1, col], e0[i, col], e0[i + 1, col] = 0.125, 0.75, 0.125
        else:
            e0[i, col], e0[i + 1, col] = 0.5, 0.5
    c["e0"] = bf(e0)
    er0 = -blocks(expand_rows(32), 4)
    c["d0"] = bf(np.concatenate([np.eye(256), er0, er0], axis=1))
    hi = np.zeros((3, 64, 640))
    lo = np.zeros((3, 64, 640))
    for first in range(3):
        up = np.eye(64)
        for k in (1, 2, 3, 4, 5):
            h = 32 >> k
            if k > 1:
                up = up @ expand_rows(4 * h)
            place = np.zeros((4 * h, 2 * h))
            place[first * h : first * h + 2 * h] = np.eye(2 * h)
            m = np.tile(up @ place, (1, 4))
            a, b = split(m)
            s = 128 * (k - 1)
            hi[first, :, s : s + m.shape[1]] = a.astype(np.float64)
            lo[first, :, s : s + m.shape[1]] = b.astype(np.float64)
    c["lb"] = bf(hi)
    c["lb5"] = bf(lo[:, :, 384:])
    assert not lo[:, :, :384].any()
    pm = np.full((8, 640), -1.0)
    for k in (1, 2, 3, 4, 5):
        for p in range(4):
            s = 128 * (k - 1) + p * ROWS[k]
            pm[:, s : s + ROWS[k]] = p
    c["pm"] = pm.astype(np.float32)
    return c


NAMES = ("v1", "wred", "v25", "h35", "er1", "er2", "er3", "er4", "ec1", "ec2", "ec3", "ec4", "e0", "d0", "lb", "lb5", "pm")


def dot(a, b):
    return jnp.dot(a, b, preferred_element_type=F32)


def halves(x):
    hi = x.astype(BF)
    return hi, (x - hi.astype(F32)).astype(BF)


def kernel(n_strip, n_lvl, offsets, photos, seams, v1, wred, v25, h35, er1, er2, er3, er4, ec1, ec2, ec3, ec4, e0, d0, lb, lb5, pm,
           out, s0, s1, tm, g1, ys, y2, c1h, c1l, send2, sendd, keep, relay, r1, r2, r3,
           halo_send, halo_recv, m1_send, m1_recv, m2_send, m2_recv, m3_send, m3_recv):
    x = lax.axis_index("strip")
    me = lax.axis_index("lvl")
    right, left = lax.rem(me + 1, n_lvl), lax.rem(me + n_lvl - 1, n_lvl)
    up, down = lax.rem(x + 1, n_strip), lax.rem(x + n_strip - 1, n_strip)
    barrier = pltpu.get_barrier_semaphore()
    for target in ({"lvl": left}, {"lvl": right}, {"strip": up}, {"strip": down}):
        pl.semaphore_signal(barrier, inc=1, device_id=target, device_id_type=MESH)

    r_i = lax.broadcasted_iota(jnp.int32, (64, 64), 0)
    c_i = lax.broadcasted_iota(jnp.int32, (64, 64), 1)
    eye = r_i == c_i
    for p in range(4):
        for e, dst in ((0, s0), (1, s1)):
            line = seams[p, e : e + 1, :].astype(F32)
            col = jnp.sum(jnp.where(eye, line, 0.0), axis=1, keepdims=True)
            dst[64 * p : 64 * p + 64, :] = jnp.broadcast_to(col, (64, 128))

    first_col = (me * N).astype(F32)

    def mask_tile(start):
        col = lax.broadcasted_iota(jnp.int32, (256, 128), 1).astype(F32) + (first_col + (start - HALO))
        return (col >= s0[...]) & (col < s1[...])

    def rows_of(ch, start, width):
        return photos[:, ch, :, start : start + width].reshape(256, width)

    lead = v1[...]
    for start in (0, N - 128):
        for ch in range(3):
            tm[ch, :, HALO + start : HALO + start + 128] = dot(lead, rows_of(ch, start, 128)).astype(BF)
    pl.semaphore_wait(barrier, 4)
    halo = []
    for i, (src, dst, target) in enumerate(((HALO, HALO + N, left), (N, 0, right))):
        copy = pltpu.make_async_remote_copy(
            src_ref=tm.at[0:3, :, src : src + 128],
            dst_ref=tm.at[0:3, :, dst : dst + 128],
            send_sem=halo_send.at[i],
            recv_sem=halo_recv.at[i],
            device_id={"lvl": target},
            device_id_type=MESH,
        )
        copy.start()
        halo.append(copy)
    for ch in range(3):
        tm[ch, :, 256 : N] = dot(lead, rows_of(ch, 128, N - 256)).astype(BF)
    for start in range(0, N + 256, 128):
        m = jnp.where(mask_tile(start), 1.0, 0.0).astype(BF)
        tm[3, :, start : start + 128] = dot(lead, m).astype(BF)

    def g1_tile(j):
        a, b = max(0, 2 * j - 1), min(10, 2 * j + 3)
        w = wred[128 * (a - 2 * j + 1) : 128 * (b - 2 * j + 1), :]
        val = dot(tm[:, :, 128 * a : 128 * b].reshape(512, 128 * (b - a)), w)
        if j in (0, 4):
            col = lax.broadcasted_iota(jnp.int32, (1, 128), 1) + (128 * j - 64) + me * (N // 2)
            val = jnp.where((col >= 0) & (col < n_lvl * (N // 2)), val, 0.0)
        g1[:, 128 * j : 128 * j + 128] = val.astype(BF)

    for j in (1, 2, 3):
        g1_tile(j)
    for copy in halo:
        copy.wait()

    @pl.when(me == 0)
    def _():
        tm[0:3, :, 0:128] = jnp.zeros((3, 128, 128), BF)

    @pl.when(me == n_lvl - 1)
    def _():
        tm[0:3, :, N + 128 : N + 256] = jnp.zeros((3, 128, 128), BF)

    for j in (0, 4):
        g1_tile(j)

    for ch in range(4):
        ys[128 * ch : 128 * ch + 128, :] = dot(v25[...], g1[128 * ch : 128 * ch + 128, :]).astype(BF)
    col = lax.broadcasted_iota(jnp.int32, (1, 384), 1) - 32 + me * (N // 4)
    inside = (col >= 0) & (col < n_lvl * (N // 4))
    for j, a, b in ((0, 0, 3), (1, 1, 5), (2, 3, 5)):
        w = wred[128 * (a - 2 * j + 1) : 128 * (b - 2 * j + 1), :]
        val = dot(ys[:, 128 * a : 128 * b], w)
        y2[:, 128 * j : 128 * j + 128] = jnp.where(inside[:, 128 * j : 128 * j + 128], val, 0.0).astype(BF)
    edge = jnp.where(me == 0, 0, jnp.where(me == n_lvl - 1, 2, 1))
    y = y2[...].reshape(4, 128, 384)
    g2 = y[:, 0:64].reshape(256, 384)
    y35 = dot(y[:, 64:128].reshape(256, 384), h35[edge]).astype(BF).reshape(4, 64, 384)
    g3 = y35[:, 0:32, 0:256].reshape(128, 256)
    g4 = y35[:, 32:48, 256:384].reshape(64, 128)
    g5 = y35[:, 48:64, 256:384].reshape(64, 128)
    gs = {1: g1[...], 2: g2, 3: g3, 4: g4, 5: g5}

    weighted = {}
    for k, er, ec, color in ((4, er4, ec4, 48), (3, er3, ec3, 48), (2, er2, ec2, 96), (1, er1, ec1, 192)):
        tall = 4 * ROWS[k]
        u_hi, u_lo = halves(dot(er[...], gs[k + 1][0:color]))
        expanded = dot(jnp.concatenate([u_hi, u_lo], axis=0), ec[...])
        half = 3 * tall
        g = gs[k].astype(F32)
        detail = g[0:half] - (expanded[0:half] + expanded[half:])
        m = g[half:]
        weighted[k] = [(m * detail[ch * tall : ch * tall + tall]).astype(BF) for ch in range(3)]
    g = g5.astype(F32)
    weighted[5] = [(g[48:64] * g[16 * ch : 16 * ch + 16]).astype(BF) for ch in range(3)]

    places = [offsets[p].astype(F32) for p in range(4)]

    def by_photo(which):
        got = jnp.zeros(which.shape, F32)
        for p in range(4):
            got = jnp.where(which == float(p), places[p], got)
        return got

    spot = by_photo(pm[0:1, :])
    table = sum(jnp.where(spot == float(o), lb[o].astype(F32), 0.0) for o in range(3)).astype(BF)
    fine = sum(jnp.where(spot[:, 384:] == float(o), lb5[o].astype(F32), 0.0) for o in range(3)).astype(BF)
    placed = {}
    for k in (5, 4, 3, 2, 1):
        s = 128 * (k - 1)
        size = {1: 128, 2: 64, 3: 32, 4: 16, 5: 16}[k]
        lhs = table[:, s : s + size]
        if k >= 4:
            lhs = jnp.concatenate([lhs, fine[:, s - 384 : s - 384 + size]], axis=0)
        parts = []
        for ch in range(3):
            got = dot(lhs, weighted[k][ch])
            parts.append(got[0:64] + got[64:128] if k >= 4 else got)
        placed[k] = jnp.concatenate(parts, axis=0)

    total = placed[5]
    for k, ec in ((4, ec4), (3, ec3), (2, ec2), (1, ec1)):
        hi, lo = halves(total)
        got = dot(jnp.concatenate([hi, lo], axis=0), ec[...])
        col = lax.broadcasted_iota(jnp.int32, (1, PAD[k]), 1) - (HALO >> k) + me * (N >> k)
        ok = (col >= 0) & (col < n_lvl * (N >> k))
        total = placed[k] + jnp.where(ok, got[0:192] + got[192:384], 0.0)
    hi, lo = halves(total)
    c1h[...] = hi
    c1l[...] = lo

    def strip_rows(width):
        q = lax.broadcasted_iota(jnp.int32, (128, width), 0)
        return ((q >> 5) + x) % 4 * 32 + (q & 31)

    lane = lax.broadcasted_iota(jnp.int32, (128, 256), 1)
    where = by_photo((lane >> 6).astype(F32)).astype(jnp.int32) * 32 + (lane & 63)
    put = jnp.where(strip_rows(256) == where, 1.0, 0.0).astype(BF)
    row = strip_rows(128)
    d = (lax.broadcasted_iota(jnp.int32, (128, 128), 1) & 63) - (row >> 1)
    even = jnp.where(d == 0, 0.75, jnp.where((d == 1) | (d == -1), 0.125, 0.0))
    odd = jnp.where((d == 0) | (d == 1), 0.5, 0.0)
    last = jnp.concatenate([put, jnp.where((row & 1) == 0, even, odd).astype(BF)], axis=1)

    def remote(src, dst, send, recv, target):
        copy = pltpu.make_async_remote_copy(
            src_ref=src, dst_ref=dst, send_sem=send, recv_sem=recv, device_id={"strip": target}, device_id_type=MESH
        )
        copy.start()
        return copy

    order = (0, 2, 1, 3)
    first, direct, second = {}, {}, {}

    def pass_on(t):
        first[t].wait_recv()
        relay[t] = (keep[t] + r1[t].astype(F32)).astype(BF)
        second[t] = remote(relay.at[t], r2.at[t], m2_send.at[t], m2_recv.at[t], up if t < 2 else down)

    for i, t in enumerate(order):
        cols = slice(128 * t, 128 * t + 256)
        lhs = jnp.concatenate([g1[0:384, cols], c1h[:, cols], c1l[:, cols]], axis=0)
        wide = dot(lhs, e0[...])
        u_hi, u_lo = halves(wide[0:384])
        b_hi, b_lo = halves(wide[384:576] + wide[576:768])
        inside = jnp.concatenate([mask_tile(HALO + 256 * t), mask_tile(HALO + 256 * t + 128)], axis=1)
        for ch in range(3):
            r = slice(128 * ch, 128 * ch + 128)
            rhs = jnp.concatenate([rows_of(ch, 256 * t, 256), u_hi[r], u_lo[r]], axis=0)
            band = jnp.where(inside, dot(d0[...], rhs), 0.0).astype(BF)
            r = slice(64 * ch, 64 * ch + 64)
            got = dot(last, jnp.concatenate([band, b_hi[r], b_lo[r]], axis=0))
            out[ch, :, 256 * t : 256 * t + 256] = got[0:32]
            rr = slice(32 * ch, 32 * ch + 32)
            send2[t, rr, :] = got[64:96].astype(BF)
            via, away = (got[32:64], got[96:128]) if t < 2 else (got[96:128], got[32:64])
            keep[t, rr, :] = via
            sendd[t, rr, :] = away.astype(BF)
        forward, back = (up, down) if t < 2 else (down, up)
        first[t] = remote(send2.at[t], r1.at[t], m1_send.at[t], m1_recv.at[t], forward)
        direct[t] = remote(sendd.at[t], r3.at[t], m3_send.at[t], m3_recv.at[t], back)
        if i > 0:
            pass_on(order[i - 1])
    pass_on(order[-1])
    for t in order:
        direct[t].wait_recv()
        second[t].wait_recv()
        got = r2[t].astype(F32) + r3[t].astype(F32)
        for ch in range(3):
            c = slice(256 * t, 256 * t + 256)
            out[ch, :, c] = out[ch, :, c] + got[32 * ch : 32 * ch + 32]
    for t in order:
        first[t].wait_send()
        direct[t].wait_send()
        second[t].wait_send()


def solution(mesh):
    n_strip, n_lvl = mesh.shape["strip"], mesh.shape["lvl"]
    table = constants()

    def per_device(photos, seams, offsets):
        vm = pl.BlockSpec(memory_space=pltpu.VMEM)
        dma = pltpu.SemaphoreType.DMA
        tile = (4, 96, 256)
        return pl.pallas_call(
            functools.partial(kernel, n_strip, n_lvl),
            out_shape=jax.ShapeDtypeStruct((3, 32, N), F32),
            in_specs=[pl.BlockSpec(memory_space=pltpu.SMEM)] + [vm] * (2 + len(NAMES)),
            out_specs=vm,
            scratch_shapes=[
                pltpu.VMEM((256, 128), F32),
                pltpu.VMEM((256, 128), F32),
                pltpu.VMEM((4, 128, 1280), BF),
                pltpu.VMEM((512, 640), BF),
                pltpu.VMEM((512, 640), BF),
                pltpu.VMEM((512, 384), BF),
                pltpu.VMEM((192, 640), BF),
                pltpu.VMEM((192, 640), BF),
                pltpu.VMEM(tile, BF),
                pltpu.VMEM(tile, BF),
                pltpu.VMEM(tile, F32),
                pltpu.VMEM(tile, BF),
                pltpu.VMEM(tile, BF),
                pltpu.VMEM(tile, BF),
                pltpu.VMEM(tile, BF),
                dma((2,)), dma((2,)), dma((4,)), dma((4,)), dma((4,)), dma((4,)), dma((4,)), dma((4,)),
            ],
            compiler_params=pltpu.CompilerParams(collective_id=0, has_side_effects=True, vmem_limit_bytes=50 << 20),
        )(offsets, photos, seams, *[jnp.asarray(table[name]) for name in NAMES])

    placed = (P("strip", None, None, "lvl"), P("strip", None, None), P("strip"))
    return jax.shard_map(
        per_device, mesh=mesh, in_specs=placed, out_specs=P(None, "strip", "lvl"), check_vma=False
    )
```

```python
import functools

import jax
import jax.numpy as jnp
import ml_dtypes
import numpy as np
from jax import lax
from jax.experimental import pallas as pl
from jax.experimental.pallas import tpu as pltpu
from jax.sharding import PartitionSpec as P

BF = jnp.bfloat16
F32 = jnp.float32
MESH = pl.DeviceIdType.MESH
TAPS = (0.0625, 0.25, 0.375, 0.25, 0.0625)
N = 1024
HALO = 128
WIDE = {0: 1280, 1: 640, 2: 320, 3: 160, 4: 80, 5: 40}
PAD = {1: 640, 2: 384, 3: 256, 4: 128, 5: 128}
ROWS = {0: 64, 1: 32, 2: 16, 3: 8, 4: 4, 5: 2}
SLOT = {2: (0, 64), 3: (64, 32), 4: (96, 16), 5: (112, 16)}


def reduce_rows(tall):
    m = np.zeros((tall // 2, tall))
    for i in range(tall // 2):
        for t in range(5):
            r = 2 * i + t - 2
            if 0 <= r < tall:
                m[i, r] = TAPS[t]
    return m


def expand_rows(tall):
    m = np.zeros((2 * tall, tall))
    for i in range(tall):
        for r, w in ((i - 1, 0.125), (i, 0.75), (i + 1, 0.125)):
            if 0 <= r < tall:
                m[2 * i, r] = w
        for r in (i, i + 1):
            if r < tall:
                m[2 * i + 1, r] = 0.5
    return m


def blocks(m, count):
    return np.kron(np.eye(count), m)


def bf(x):
    return np.asarray(x, np.float32).astype(ml_dtypes.bfloat16)


def split(x):
    hi = bf(x)
    return hi, bf(np.asarray(x, np.float64) - hi.astype(np.float64))


def valid(level, edge):
    e = np.arange(WIDE[level])
    h = HALO >> level
    n = N >> level
    keep = np.ones(WIDE[level])
    if edge == 0:
        keep[e < h] = 0
    if edge == 2:
        keep[e >= h + n] = 0
    return keep


def reduce_cols(level, edge):
    m = reduce_rows(WIDE[level]).T
    return m * valid(level + 1, edge)[None, :]


def constants():
    c = {}
    c["v1"] = bf(blocks(reduce_rows(64), 4))
    w = np.zeros((512, 128))
    for col in range(128):
        for t in range(5):
            w[128 + 2 * col + t - 2, col] = TAPS[t]
    c["wred"] = bf(w)
    v = {1: np.eye(32)}
    for k in (2, 3, 4, 5):
        v[k] = reduce_rows(ROWS[k - 1]) @ v[k - 1]
    v25 = np.zeros((128, 128))
    for k in (2, 3, 4, 5):
        start, _ = SLOT[k]
        v25[start : start + 4 * ROWS[k]] = blocks(v[k], 4)
    c["v25"] = bf(v25)
    h35 = np.zeros((3, 384, 384))
    for edge in range(3):
        m3 = reduce_cols(2, edge)
        m4 = m3 @ reduce_cols(3, edge)
        m5 = m4 @ reduce_cols(4, edge)
        h35[edge, :320, 0:160] = m3
        h35[edge, :320, 256:336] = m4
        h35[edge, :320, 336:376] = m5
    c["h35"] = bf(h35)
    c["er1"] = bf(blocks(expand_rows(16), 12))
    c["er2"] = bf(blocks(expand_rows(8), 12))
    c["er3"] = bf(blocks(expand_rows(4), 12))
    er4 = np.zeros((48, 48))
    for ch in range(3):
        er4[16 * ch : 16 * ch + 16, 16 * ch : 16 * ch + 8] = blocks(expand_rows(2), 4)
    c["er4"] = bf(er4)
    for k in (1, 2, 3, 4):
        m = np.zeros((PAD[k + 1], PAD[k]))
        at = 80 if k == 4 else 0
        m[at : at + WIDE[k + 1], : WIDE[k]] = expand_rows(WIDE[k + 1]).T
        c[f"ec{k}"] = bf(m)
    e0 = np.zeros((256, 256))
    for col in range(256):
        i = 64 + col // 2
        if col % 2 == 0:
            e0[i - 1, col], e0[i, col], e0[i + 1, col] = 0.125, 0.75, 0.125
        else:
            e0[i, col], e0[i + 1, col] = 0.5, 0.5
    c["e0"] = bf(e0)
    er0 = -blocks(expand_rows(32), 4)
    c["d0"] = bf(np.concatenate([np.eye(256), er0, er0], axis=1))
    hi = np.zeros((3, 64, 640))
    lo = np.zeros((3, 64, 640))
    for first in range(3):
        up = np.eye(64)
        for k in (1, 2, 3, 4, 5):
            h = 32 >> k
            if k > 1:
                up = up @ expand_rows(4 * h)
            place = np.zeros((4 * h, 2 * h))
            place[first * h : first * h + 2 * h] = np.eye(2 * h)
            m = np.tile(up @ place, (1, 4))
            a, b = split(m)
            s = 128 * (k - 1)
            hi[first, :, s : s + m.shape[1]] = a.astype(np.float64)
            lo[first, :, s : s + m.shape[1]] = b.astype(np.float64)
    c["lb"] = bf(hi)
    c["lb5"] = bf(lo[:, :, 384:])
    assert not lo[:, :, :384].any()
    pm = np.full((8, 640), -1.0)
    for k in (1, 2, 3, 4, 5):
        for p in range(4):
            s = 128 * (k - 1) + p * ROWS[k]
            pm[:, s : s + ROWS[k]] = p
    c["pm"] = pm.astype(np.float32)
    return c


NAMES = ("v1", "wred", "v25", "h35", "er1", "er2", "er3", "er4", "ec1", "ec2", "ec3", "ec4", "e0", "d0", "lb", "lb5", "pm")


def dot(a, b):
    return jnp.dot(a, b, preferred_element_type=F32)


def halves(x):
    hi = x.astype(BF)
    return hi, (x - hi.astype(F32)).astype(BF)


def kernel(n_strip, n_lvl, offsets, photos_in, seams, *refs):
    given, out, held, rest = refs[: len(NAMES)], refs[len(NAMES)], refs[len(NAMES) + 1 : 2 * len(NAMES) + 1], refs[2 * len(NAMES) + 1 :]
    body(n_strip, n_lvl, offsets, photos_in, seams, dict(zip(NAMES, given)), out, dict(zip(NAMES, held)), *rest)


def body(n_strip, n_lvl, offsets, photos_in, seams, given, out, held, load, photos, s0, s1, tm, g1, ys, y2, c1h, c1l, send2, sendd, keep, relay, r1, r2, r3,
         halo_send, halo_recv, m1_send, m1_recv, m2_send, m2_recv, m3_send, m3_recv):
    x = lax.axis_index("strip")
    me = lax.axis_index("lvl")
    edge = jnp.where(me == 0, 0, jnp.where(me == n_lvl - 1, 2, 1))
    waits = {}

    def fetch(name, src, dst):
        copy = pltpu.make_async_copy(src, dst, load.at[len(waits)])
        copy.start()
        waits[name] = copy

    def ready(name):
        if waits[name] is not None:
            waits[name].wait()
            waits[name] = None

    def const(name):
        ready(name)
        return held[name]

    fetch("v1", given["v1"], held["v1"])
    for ch in range(3):
        fetch(ch, photos_in.at[:, ch], photos.at[:, ch])
    for name in NAMES[1:]:
        fetch(name, given[name].at[edge] if name == "h35" else given[name], held[name])

    right, left = lax.rem(me + 1, n_lvl), lax.rem(me + n_lvl - 1, n_lvl)
    up, down = lax.rem(x + 1, n_strip), lax.rem(x + n_strip - 1, n_strip)
    barrier = pltpu.get_barrier_semaphore()
    for target in ({"lvl": left}, {"lvl": right}, {"strip": up}, {"strip": down}):
        pl.semaphore_signal(barrier, inc=1, device_id=target, device_id_type=MESH)

    r_i = lax.broadcasted_iota(jnp.int32, (64, 64), 0)
    c_i = lax.broadcasted_iota(jnp.int32, (64, 64), 1)
    eye = r_i == c_i
    for p in range(4):
        for e, dst in ((0, s0), (1, s1)):
            line = seams[p, e : e + 1, :].astype(F32)
            col = jnp.sum(jnp.where(eye, line, 0.0), axis=1, keepdims=True)
            dst[64 * p : 64 * p + 64, :] = jnp.broadcast_to(col, (64, 128))

    first_col = (me * N).astype(F32)

    def mask_tile(start):
        col = lax.broadcasted_iota(jnp.int32, (256, 128), 1).astype(F32) + (first_col + (start - HALO))
        return (col >= s0[...]) & (col < s1[...])

    def rows_of(ch, start, width):
        return photos[:, ch, :, start : start + width].reshape(256, width)

    lead = const("v1")[...]
    for ch in range(3):
        ready(ch)
    for start in (0, N - 128):
        for ch in range(3):
            tm[ch, :, HALO + start : HALO + start + 128] = dot(lead, rows_of(ch, start, 128)).astype(BF)
    pl.semaphore_wait(barrier, 4)
    halo = []
    for i, (src, dst, target) in enumerate(((HALO, HALO + N, left), (N, 0, right))):
        copy = pltpu.make_async_remote_copy(
            src_ref=tm.at[0:3, :, src : src + 128],
            dst_ref=tm.at[0:3, :, dst : dst + 128],
            send_sem=halo_send.at[i],
            recv_sem=halo_recv.at[i],
            device_id={"lvl": target},
            device_id_type=MESH,
        )
        copy.start()
        halo.append(copy)
    for ch in range(3):
        tm[ch, :, 256 : N] = dot(lead, rows_of(ch, 128, N - 256)).astype(BF)
    for start in range(0, N + 256, 128):
        m = jnp.where(mask_tile(start), 1.0, 0.0).astype(BF)
        tm[3, :, start : start + 128] = dot(lead, m).astype(BF)

    wred = const("wred")

    def g1_tile(j):
        a, b = max(0, 2 * j - 1), min(10, 2 * j + 3)
        w = wred[128 * (a - 2 * j + 1) : 128 * (b - 2 * j + 1), :]
        val = dot(tm[:, :, 128 * a : 128 * b].reshape(512, 128 * (b - a)), w)
        if j in (0, 4):
            col = lax.broadcasted_iota(jnp.int32, (1, 128), 1) + (128 * j - 64) + me * (N // 2)
            val = jnp.where((col >= 0) & (col < n_lvl * (N // 2)), val, 0.0)
        g1[:, 128 * j : 128 * j + 128] = val.astype(BF)

    for j in (1, 2, 3):
        g1_tile(j)
    for copy in halo:
        copy.wait()

    @pl.when(me == 0)
    def _():
        tm[0:3, :, 0:128] = jnp.zeros((3, 128, 128), BF)

    @pl.when(me == n_lvl - 1)
    def _():
        tm[0:3, :, N + 128 : N + 256] = jnp.zeros((3, 128, 128), BF)

    for j in (0, 4):
        g1_tile(j)

    for ch in range(4):
        ys[128 * ch : 128 * ch + 128, :] = dot(const("v25")[...], g1[128 * ch : 128 * ch + 128, :]).astype(BF)
    col = lax.broadcasted_iota(jnp.int32, (1, 384), 1) - 32 + me * (N // 4)
    inside = (col >= 0) & (col < n_lvl * (N // 4))
    for j, a, b in ((0, 0, 3), (1, 1, 5), (2, 3, 5)):
        w = wred[128 * (a - 2 * j + 1) : 128 * (b - 2 * j + 1), :]
        val = dot(ys[:, 128 * a : 128 * b], w)
        y2[:, 128 * j : 128 * j + 128] = jnp.where(inside[:, 128 * j : 128 * j + 128], val, 0.0).astype(BF)
    y = y2[...].reshape(4, 128, 384)
    g2 = y[:, 0:64].reshape(256, 384)
    y35 = dot(y[:, 64:128].reshape(256, 384), const("h35")[...]).astype(BF).reshape(4, 64, 384)
    g3 = y35[:, 0:32, 0:256].reshape(128, 256)
    g4 = y35[:, 32:48, 256:384].reshape(64, 128)
    g5 = y35[:, 48:64, 256:384].reshape(64, 128)
    gs = {1: g1[...], 2: g2, 3: g3, 4: g4, 5: g5}

    weighted = {}
    er = {k: const(f"er{k}") for k in (1, 2, 3, 4)}
    ec = {k: const(f"ec{k}") for k in (1, 2, 3, 4)}
    for k, color in ((4, 48), (3, 48), (2, 96), (1, 192)):
        tall = 4 * ROWS[k]
        u_hi, u_lo = halves(dot(er[k][...], gs[k + 1][0:color]))
        expanded = dot(jnp.concatenate([u_hi, u_lo], axis=0), ec[k][...])
        half = 3 * tall
        g = gs[k].astype(F32)
        detail = g[0:half] - (expanded[0:half] + expanded[half:])
        m = g[half:]
        weighted[k] = [(m * detail[ch * tall : ch * tall + tall]).astype(BF) for ch in range(3)]
    g = g5.astype(F32)
    weighted[5] = [(g[48:64] * g[16 * ch : 16 * ch + 16]).astype(BF) for ch in range(3)]

    pm, lb, lb5 = const("pm"), const("lb"), const("lb5")
    places = [offsets[p].astype(F32) for p in range(4)]

    def by_photo(which):
        got = jnp.zeros(which.shape, F32)
        for p in range(4):
            got = jnp.where(which == float(p), places[p], got)
        return got

    spot = by_photo(pm[0:1, :])
    table = sum(jnp.where(spot == float(o), lb[o].astype(F32), 0.0) for o in range(3)).astype(BF)
    fine = sum(jnp.where(spot[:, 384:] == float(o), lb5[o].astype(F32), 0.0) for o in range(3)).astype(BF)
    placed = {}
    for k in (5, 4, 3, 2, 1):
        s = 128 * (k - 1)
        size = {1: 128, 2: 64, 3: 32, 4: 16, 5: 16}[k]
        lhs = table[:, s : s + size]
        if k >= 4:
            lhs = jnp.concatenate([lhs, fine[:, s - 384 : s - 384 + size]], axis=0)
        parts = []
        for ch in range(3):
            got = dot(lhs, weighted[k][ch])
            parts.append(got[0:64] + got[64:128] if k >= 4 else got)
        placed[k] = jnp.concatenate(parts, axis=0)

    total = placed[5]
    for k in (4, 3, 2, 1):
        hi, lo = halves(total)
        got = dot(jnp.concatenate([hi, lo], axis=0), ec[k][...])
        col = lax.broadcasted_iota(jnp.int32, (1, PAD[k]), 1) - (HALO >> k) + me * (N >> k)
        ok = (col >= 0) & (col < n_lvl * (N >> k))
        total = placed[k] + jnp.where(ok, got[0:192] + got[192:384], 0.0)
    hi, lo = halves(total)
    c1h[...] = hi
    c1l[...] = lo

    def strip_rows(width):
        q = lax.broadcasted_iota(jnp.int32, (128, width), 0)
        return ((q >> 5) + x) % 4 * 32 + (q & 31)

    lane = lax.broadcasted_iota(jnp.int32, (128, 256), 1)
    where = by_photo((lane >> 6).astype(F32)).astype(jnp.int32) * 32 + (lane & 63)
    put = jnp.where(strip_rows(256) == where, 1.0, 0.0).astype(BF)
    row = strip_rows(128)
    d = (lax.broadcasted_iota(jnp.int32, (128, 128), 1) & 63) - (row >> 1)
    even = jnp.where(d == 0, 0.75, jnp.where((d == 1) | (d == -1), 0.125, 0.0))
    odd = jnp.where((d == 0) | (d == 1), 0.5, 0.0)
    last = jnp.concatenate([put, jnp.where((row & 1) == 0, even, odd).astype(BF)], axis=1)

    def remote(src, dst, send, recv, target):
        copy = pltpu.make_async_remote_copy(
            src_ref=src, dst_ref=dst, send_sem=send, recv_sem=recv, device_id={"strip": target}, device_id_type=MESH
        )
        copy.start()
        return copy

    order = (0, 2, 1, 3)
    e0, d0 = const("e0"), const("d0")
    first, direct, second = {}, {}, {}

    def pass_on(t):
        first[t].wait_recv()
        relay[t] = (keep[t] + r1[t].astype(F32)).astype(BF)
        second[t] = remote(relay.at[t], r2.at[t], m2_send.at[t], m2_recv.at[t], up if t < 2 else down)

    for i, t in enumerate(order):
        cols = slice(128 * t, 128 * t + 256)
        lhs = jnp.concatenate([g1[0:384, cols], c1h[:, cols], c1l[:, cols]], axis=0)
        wide = dot(lhs, e0[...])
        u_hi, u_lo = halves(wide[0:384])
        b_hi, b_lo = halves(wide[384:576] + wide[576:768])
        inside = jnp.concatenate([mask_tile(HALO + 256 * t), mask_tile(HALO + 256 * t + 128)], axis=1)
        for ch in range(3):
            r = slice(128 * ch, 128 * ch + 128)
            rhs = jnp.concatenate([rows_of(ch, 256 * t, 256), u_hi[r], u_lo[r]], axis=0)
            band = jnp.where(inside, dot(d0[...], rhs), 0.0).astype(BF)
            r = slice(64 * ch, 64 * ch + 64)
            got = dot(last, jnp.concatenate([band, b_hi[r], b_lo[r]], axis=0))
            out[ch, :, 256 * t : 256 * t + 256] = got[0:32]
            rr = slice(32 * ch, 32 * ch + 32)
            send2[t, rr, :] = got[64:96].astype(BF)
            via, away = (got[32:64], got[96:128]) if t < 2 else (got[96:128], got[32:64])
            keep[t, rr, :] = via
            sendd[t, rr, :] = away.astype(BF)
        forward, back = (up, down) if t < 2 else (down, up)
        first[t] = remote(send2.at[t], r1.at[t], m1_send.at[t], m1_recv.at[t], forward)
        direct[t] = remote(sendd.at[t], r3.at[t], m3_send.at[t], m3_recv.at[t], back)
        if i > 0:
            pass_on(order[i - 1])
    pass_on(order[-1])
    for t in order:
        direct[t].wait_recv()
        second[t].wait_recv()
        got = r2[t].astype(F32) + r3[t].astype(F32)
        for ch in range(3):
            c = slice(256 * t, 256 * t + 256)
            out[ch, :, c] = out[ch, :, c] + got[32 * ch : 32 * ch + 32]
    for t in order:
        first[t].wait_send()
        direct[t].wait_send()
        second[t].wait_send()


def solution(mesh):
    n_strip, n_lvl = mesh.shape["strip"], mesh.shape["lvl"]
    table = constants()

    def per_device(photos, seams, offsets):
        vm = pl.BlockSpec(memory_space=pltpu.VMEM)
        far = pl.BlockSpec(memory_space=pltpu.HBM)
        given = [jnp.asarray(table[name]) for name in NAMES]
        dma = pltpu.SemaphoreType.DMA
        tile = (4, 96, 256)
        return pl.pallas_call(
            functools.partial(kernel, n_strip, n_lvl),
            out_shape=jax.ShapeDtypeStruct((3, 32, N), F32),
            in_specs=[pl.BlockSpec(memory_space=pltpu.SMEM), far, vm] + [far] * len(NAMES),
            out_specs=vm,
            scratch_shapes=[
                *[pltpu.VMEM(a.shape[1:] if name == "h35" else a.shape, a.dtype) for name, a in zip(NAMES, given)],
                dma((len(NAMES) + 3,)),
                pltpu.VMEM((4, 3, 64, N), BF),
                pltpu.VMEM((256, 128), F32),
                pltpu.VMEM((256, 128), F32),
                pltpu.VMEM((4, 128, 1280), BF),
                pltpu.VMEM((512, 640), BF),
                pltpu.VMEM((512, 640), BF),
                pltpu.VMEM((512, 384), BF),
                pltpu.VMEM((192, 640), BF),
                pltpu.VMEM((192, 640), BF),
                pltpu.VMEM(tile, BF),
                pltpu.VMEM(tile, BF),
                pltpu.VMEM(tile, F32),
                pltpu.VMEM(tile, BF),
                pltpu.VMEM(tile, BF),
                pltpu.VMEM(tile, BF),
                pltpu.VMEM(tile, BF),
                dma((2,)), dma((2,)), dma((4,)), dma((4,)), dma((4,)), dma((4,)), dma((4,)), dma((4,)),
            ],
            compiler_params=pltpu.CompilerParams(collective_id=0, has_side_effects=True),
        )(offsets, photos, seams, *given)

    placed = (P("strip", None, None, "lvl"), P("strip", None, None), P("strip"))
    return jax.shard_map(
        per_device, mesh=mesh, in_specs=placed, out_specs=P(None, "strip", "lvl"), check_vma=False
    )
```

```python
import functools

import jax
import jax.numpy as jnp
import ml_dtypes
import numpy as np
from jax import lax
from jax.experimental import pallas as pl
from jax.experimental.pallas import tpu as pltpu
from jax.sharding import PartitionSpec as P

BF = jnp.bfloat16
F32 = jnp.float32
MESH = pl.DeviceIdType.MESH
TAPS = (0.0625, 0.25, 0.375, 0.25, 0.0625)
N = 1024
HALO = 128
WIDE = {0: 1280, 1: 640, 2: 320, 3: 160, 4: 80, 5: 40}
PAD = {1: 640, 2: 384, 3: 256, 4: 128, 5: 128}
ROWS = {0: 64, 1: 32, 2: 16, 3: 8, 4: 4, 5: 2}
SLOT = {2: (0, 64), 3: (64, 32), 4: (96, 16), 5: (112, 16)}


def reduce_rows(tall):
    m = np.zeros((tall // 2, tall))
    for i in range(tall // 2):
        for t in range(5):
            r = 2 * i + t - 2
            if 0 <= r < tall:
                m[i, r] = TAPS[t]
    return m


def expand_rows(tall):
    m = np.zeros((2 * tall, tall))
    for i in range(tall):
        for r, w in ((i - 1, 0.125), (i, 0.75), (i + 1, 0.125)):
            if 0 <= r < tall:
                m[2 * i, r] = w
        for r in (i, i + 1):
            if r < tall:
                m[2 * i + 1, r] = 0.5
    return m


def blocks(m, count):
    return np.kron(np.eye(count), m)


def bf(x):
    return np.asarray(x, np.float32).astype(ml_dtypes.bfloat16)


def split(x):
    hi = bf(x)
    return hi, bf(np.asarray(x, np.float64) - hi.astype(np.float64))


def valid(level, edge):
    e = np.arange(WIDE[level])
    h = HALO >> level
    n = N >> level
    keep = np.ones(WIDE[level])
    if edge == 0:
        keep[e < h] = 0
    if edge == 2:
        keep[e >= h + n] = 0
    return keep


def reduce_cols(level, edge):
    m = reduce_rows(WIDE[level]).T
    return m * valid(level + 1, edge)[None, :]


def constants():
    c = {}
    c["v1"] = bf(blocks(reduce_rows(64), 4))
    w = np.zeros((512, 128))
    for col in range(128):
        for t in range(5):
            w[128 + 2 * col + t - 2, col] = TAPS[t]
    c["wred"] = bf(w)
    v = {1: np.eye(32)}
    for k in (2, 3, 4, 5):
        v[k] = reduce_rows(ROWS[k - 1]) @ v[k - 1]
    v25 = np.zeros((128, 128))
    for k in (2, 3, 4, 5):
        start, _ = SLOT[k]
        v25[start : start + 4 * ROWS[k]] = blocks(v[k], 4)
    c["v25"] = bf(v25)
    h35 = np.zeros((3, 384, 384))
    for edge in range(3):
        m3 = reduce_cols(2, edge)
        m4 = m3 @ reduce_cols(3, edge)
        m5 = m4 @ reduce_cols(4, edge)
        h35[edge, :320, 0:160] = m3
        h35[edge, :320, 256:336] = m4
        h35[edge, :320, 336:376] = m5
    c["h35"] = bf(h35)
    c["er1"] = bf(blocks(expand_rows(16), 12))
    c["er2"] = bf(blocks(expand_rows(8), 12))
    c["er3"] = bf(blocks(expand_rows(4), 12))
    er4 = np.zeros((48, 48))
    for ch in range(3):
        er4[16 * ch : 16 * ch + 16, 16 * ch : 16 * ch + 8] = blocks(expand_rows(2), 4)
    c["er4"] = bf(er4)
    for k in (1, 2, 3, 4):
        m = np.zeros((PAD[k + 1], PAD[k]))
        at = 80 if k == 4 else 0
        m[at : at + WIDE[k + 1], : WIDE[k]] = expand_rows(WIDE[k + 1]).T
        if k == 1:
            c["ec1a"], c["ec1b"] = bf(m[0:256, 0:384]), bf(m[128:384, 384:640])
        else:
            c[f"ec{k}"] = bf(m)
    e0 = np.zeros((256, 256))
    for col in range(256):
        i = 64 + col // 2
        if col % 2 == 0:
            e0[i - 1, col], e0[i, col], e0[i + 1, col] = 0.125, 0.75, 0.125
        else:
            e0[i, col], e0[i + 1, col] = 0.5, 0.5
    c["e0"] = bf(e0)
    er0 = blocks(expand_rows(32), 4)
    c["d0"] = bf(np.concatenate([er0, er0], axis=1))
    hi = np.zeros((3, 64, 640))
    lo = np.zeros((3, 64, 640))
    for first in range(3):
        up = np.eye(64)
        for k in (1, 2, 3, 4, 5):
            h = 32 >> k
            if k > 1:
                up = up @ expand_rows(4 * h)
            place = np.zeros((4 * h, 2 * h))
            place[first * h : first * h + 2 * h] = np.eye(2 * h)
            m = np.tile(up @ place, (1, 4))
            a, b = split(m)
            s = 128 * (k - 1)
            hi[first, :, s : s + m.shape[1]] = a.astype(np.float64)
            lo[first, :, s : s + m.shape[1]] = b.astype(np.float64)
    c["lb"] = bf(hi)
    c["lb5"] = bf(lo[:, :, 384:])
    assert not lo[:, :, :384].any()
    pm = np.full((8, 640), -1.0)
    for k in (1, 2, 3, 4, 5):
        for p in range(4):
            s = 128 * (k - 1) + p * ROWS[k]
            pm[:, s : s + ROWS[k]] = p
    c["pm"] = pm.astype(np.float32)
    return c


NAMES = ("v1", "wred", "v25", "h35", "er1", "er2", "er3", "er4", "ec1a", "ec1b", "ec2", "ec3", "ec4", "e0", "d0", "lb", "lb5", "pm")


def dot(a, b):
    return jnp.dot(a, b, preferred_element_type=F32)


def halves(x):
    hi = x.astype(BF)
    return hi, (x - hi.astype(F32)).astype(BF)


def kernel(n_strip, n_lvl, offsets_in, photos_in, seams_in, *refs):
    n = len(NAMES)
    given, (out, r2, r3), held, rest = refs[:n], refs[n : n + 3], refs[n + 3 : 2 * n + 3], refs[2 * n + 3 :]
    body(n_strip, n_lvl, offsets_in, photos_in, seams_in, dict(zip(NAMES, given)), out, r2, r3, dict(zip(NAMES, held)), *rest)


def body(n_strip, n_lvl, offsets_in, photos_in, seams_in, given, out, r2, r3, held, load, photos, offsets, seams, s0, s1, tm, g1, ys, y2, bands,
         c1h, c1l, send2, sendd, keep, relay, r1, own, own_sem,
         halo_send, halo_recv, m1_send, m1_recv, m2_send, m2_recv, m3_send, m3_recv):
    x = lax.axis_index("strip")
    me = lax.axis_index("lvl")
    right, left = lax.rem(me + 1, n_lvl), lax.rem(me + n_lvl - 1, n_lvl)
    up, down = lax.rem(x + 1, n_strip), lax.rem(x + n_strip - 1, n_strip)
    barrier = pltpu.get_barrier_semaphore()
    for target in ({"lvl": left}, {"lvl": right}, {"strip": up}, {"strip": down}):
        pl.semaphore_signal(barrier, inc=1, device_id=target, device_id_type=MESH)
    edge = jnp.where(me == 0, 0, jnp.where(me == n_lvl - 1, 2, 1))
    waits = {}

    def fetch(name, src, dst):
        copy = pltpu.make_async_copy(src, dst, load.at[len(waits)])
        copy.start()
        waits[name] = copy

    def ready(name):
        if waits[name] is not None:
            waits[name].wait()
            waits[name] = None

    def const(name):
        ready(name)
        return held[name]

    fetch("seams", seams_in, seams)
    fetch("v1", given["v1"], held["v1"])
    for ch in range(3):
        fetch(ch, photos_in.at[:, ch], photos.at[:, ch])
    fetch("offsets", offsets_in, offsets)
    for name in NAMES[1:]:
        fetch(name, given[name].at[edge] if name == "h35" else given[name], held[name])

    def rows_of(ch, start, width):
        return photos[:, ch, :, start : start + width].reshape(256, width)

    lead = const("v1")[...]
    for ch in range(3):
        ready(ch)
    for start in (0, N - 128):
        for ch in range(3):
            tm[ch, :, HALO + start : HALO + start + 128] = dot(lead, rows_of(ch, start, 128)).astype(BF)
    pl.semaphore_wait(barrier, 4)
    halo = []
    for i, (src, dst, target) in enumerate(((HALO, HALO + N, left), (N, 0, right))):
        copy = pltpu.make_async_remote_copy(
            src_ref=tm.at[0:3, :, src : src + 128],
            dst_ref=tm.at[0:3, :, dst : dst + 128],
            send_sem=halo_send.at[i],
            recv_sem=halo_recv.at[i],
            device_id={"lvl": target},
            device_id_type=MESH,
        )
        copy.start()
        halo.append(copy)
    r_i = lax.broadcasted_iota(jnp.int32, (64, 64), 0)
    c_i = lax.broadcasted_iota(jnp.int32, (64, 64), 1)
    eye = r_i == c_i
    ready("seams")
    for p in range(4):
        for e, dst in ((0, s0), (1, s1)):
            line = seams[p, e : e + 1, :].astype(F32)
            col = jnp.sum(jnp.where(eye, line, 0.0), axis=1, keepdims=True)
            dst[64 * p : 64 * p + 64, :] = jnp.broadcast_to(col, (64, 128))

    first_col = (me * N).astype(F32)

    def mask_tile(start):
        col = lax.broadcasted_iota(jnp.int32, (256, 128), 1).astype(F32) + (first_col + (start - HALO))
        a, b = s0[...], s1[...]
        return jnp.concatenate([(c >= a) & (c < b) for c in (col, col + 128.0)], axis=1)

    for ch in range(3):
        tm[ch, :, 256 : N] = dot(lead, rows_of(ch, 128, N - 256)).astype(BF)
    for start in range(0, N + 256, 256):
        m = jnp.where(mask_tile(start), 1.0, 0.0).astype(BF)
        tm[3, :, start : start + 256] = dot(lead, m).astype(BF)

    wred = const("wred")

    def g1_tile(j):
        a, b = max(0, 2 * j - 1), min(10, 2 * j + 3)
        w = wred[128 * (a - 2 * j + 1) : 128 * (b - 2 * j + 1), :]
        val = dot(tm[:, :, 128 * a : 128 * b].reshape(512, 128 * (b - a)), w)
        if j in (0, 4):
            col = lax.broadcasted_iota(jnp.int32, (1, 128), 1) + (128 * j - 64) + me * (N // 2)
            val = jnp.where((col >= 0) & (col < n_lvl * (N // 2)), val, 0.0)
        g1[:, 128 * j : 128 * j + 128] = val.astype(BF)

    for j in (1, 2, 3):
        g1_tile(j)
    e0, d0 = const("e0"), const("d0")

    def band(t, ch):
        cols = slice(128 * t, 128 * t + 256)
        u_hi, u_lo = halves(dot(g1[128 * ch : 128 * ch + 128, cols], e0[...]))
        away = dot(d0[...], jnp.concatenate([u_hi, u_lo], axis=0))
        detail = rows_of(ch, 256 * t, 256).astype(F32) - away
        bands[ch, :, 256 * t : 256 * t + 256] = jnp.where(mask_tile(HALO + 256 * t), detail, 0.0).astype(BF)

    for t in (1, 2):
        for ch in range(3):
            band(t, ch)
    for name in NAMES:
        ready(name)
    ready("offsets")
    for copy in halo:
        copy.wait()
    for at, outer in ((0, 0), (N + 128, n_lvl - 1)):
        tm[0:3, :, at : at + 128] = jnp.where(me == outer, jnp.zeros((), BF), tm[0:3, :, at : at + 128])
    for j in (0, 4):
        g1_tile(j)

    for ch in range(4):
        ys[128 * ch : 128 * ch + 128, :] = dot(const("v25")[...], g1[128 * ch : 128 * ch + 128, :]).astype(BF)
    col = lax.broadcasted_iota(jnp.int32, (1, 384), 1) - 32 + me * (N // 4)
    inside = (col >= 0) & (col < n_lvl * (N // 4))
    for j, a, b in ((0, 0, 3), (1, 1, 5), (2, 3, 5)):
        w = wred[128 * (a - 2 * j + 1) : 128 * (b - 2 * j + 1), :]
        val = dot(ys[:, 128 * a : 128 * b], w)
        y2[:, 128 * j : 128 * j + 128] = jnp.where(inside[:, 128 * j : 128 * j + 128], val, 0.0).astype(BF)
    band(0, 0)
    y = y2[...].reshape(4, 128, 384)
    g2 = y[:, 0:64].reshape(256, 384)
    y35 = dot(y[:, 64:128].reshape(256, 384), const("h35")[...]).astype(BF).reshape(4, 64, 384)
    g3 = y35[:, 0:32, 0:256].reshape(128, 256)
    g4 = y35[:, 32:48, 256:384].reshape(64, 128)
    g5 = y35[:, 48:64, 256:384].reshape(64, 128)
    band(0, 1)
    gs = {1: g1[...], 2: g2, 3: g3, 4: g4, 5: g5}

    weighted = {}
    er = {k: const(f"er{k}") for k in (1, 2, 3, 4)}

    def widen(k, field):
        if k == 1:
            return jnp.concatenate([dot(field[:, 0:256], held["ec1a"][...]), dot(field[:, 128:384], held["ec1b"][...])], axis=1)
        return dot(field, held[f"ec{k}"][...])

    for k, color in ((4, 48), (3, 48), (2, 96), (1, 192)):
        tall = 4 * ROWS[k]
        u_hi, u_lo = halves(dot(er[k][...], gs[k + 1][0:color]))
        expanded = widen(k, jnp.concatenate([u_hi, u_lo], axis=0))
        half = 3 * tall
        g = gs[k].astype(F32)
        detail = g[0:half] - (expanded[0:half] + expanded[half:])
        m = g[half:]
        weighted[k] = [(m * detail[ch * tall : ch * tall + tall]).astype(BF) for ch in range(3)]
    band(0, 2)
    g = g5.astype(F32)
    weighted[5] = [(g[48:64] * g[16 * ch : 16 * ch + 16]).astype(BF) for ch in range(3)]

    pm, lb, lb5 = const("pm"), const("lb"), const("lb5")
    places = [offsets[p].astype(F32) for p in range(4)]

    def by_photo(which):
        got = jnp.zeros(which.shape, F32)
        for p in range(4):
            got = jnp.where(which == float(p), places[p], got)
        return got

    spot = by_photo(pm[0:1, :])
    table = sum(jnp.where(spot == float(o), lb[o].astype(F32), 0.0) for o in range(3)).astype(BF)
    fine = sum(jnp.where(spot[:, 384:] == float(o), lb5[o].astype(F32), 0.0) for o in range(3)).astype(BF)
    band(3, 0)
    placed = {}
    for k in (5, 4, 3, 2, 1):
        s = 128 * (k - 1)
        size = {1: 128, 2: 64, 3: 32, 4: 16, 5: 16}[k]
        lhs = table[:, s : s + size]
        if k >= 4:
            lhs = jnp.concatenate([lhs, fine[:, s - 384 : s - 384 + size]], axis=0)
        parts = []
        for ch in range(3):
            got = dot(lhs, weighted[k][ch])
            parts.append(got[0:64] + got[64:128] if k >= 4 else got)
        placed[k] = jnp.concatenate(parts, axis=0)

    band(3, 1)

    total = placed[5]
    for k in (4, 3, 2, 1):
        hi, lo = halves(total)
        got = widen(k, jnp.concatenate([hi, lo], axis=0))
        col = lax.broadcasted_iota(jnp.int32, (1, PAD[k]), 1) - (HALO >> k) + me * (N >> k)
        ok = (col >= 0) & (col < n_lvl * (N >> k))
        total = placed[k] + jnp.where(ok, got[0:192] + got[192:384], 0.0)
    band(3, 2)
    hi, lo = halves(total)
    c1h[...] = hi
    c1l[...] = lo

    def strip_rows(width):
        q = lax.broadcasted_iota(jnp.int32, (128, width), 0)
        return ((q >> 5) + x) % 4 * 32 + (q & 31)

    lane = lax.broadcasted_iota(jnp.int32, (128, 256), 1)
    where = by_photo((lane >> 6).astype(F32)).astype(jnp.int32) * 32 + (lane & 63)
    put = jnp.where(strip_rows(256) == where, 1.0, 0.0).astype(BF)
    row = strip_rows(128)
    d = (lax.broadcasted_iota(jnp.int32, (128, 128), 1) & 63) - (row >> 1)
    even = jnp.where(d == 0, 0.75, jnp.where((d == 1) | (d == -1), 0.125, 0.0))
    odd = jnp.where((d == 0) | (d == 1), 0.5, 0.0)
    last = jnp.concatenate([put, jnp.where((row & 1) == 0, even, odd).astype(BF)], axis=1)

    def remote(src, dst, send, recv, target):
        copy = pltpu.make_async_remote_copy(
            src_ref=src, dst_ref=dst, send_sem=send, recv_sem=recv, device_id={"strip": target}, device_id_type=MESH
        )
        copy.start()
        return copy

    order = (0, 2, 1, 3)
    first, direct, second, done = {}, {}, {}, {}

    def pass_on(t):
        first[t].wait_recv()
        relay[t] = (keep[t] + r1[t].astype(F32)).astype(BF)
        cols = slice(256 * t, 256 * t + 256)
        second[t] = remote(relay.at[t], r2.at[:, :, cols], m2_send.at[t], m2_recv.at[t], up if t < 2 else down)

    for i, t in enumerate(order):
        cols = slice(128 * t, 128 * t + 256)
        wide = dot(jnp.concatenate([c1h[:, cols], c1l[:, cols]], axis=0), e0[...])
        b_hi, b_lo = halves(wide[0:192] + wide[192:384])
        cols = slice(256 * t, 256 * t + 256)
        for ch in range(3):
            r = slice(64 * ch, 64 * ch + 64)
            got = dot(last, jnp.concatenate([bands[ch, :, cols], b_hi[r], b_lo[r]], axis=0))
            own[t, ch] = got[0:32]
            send2[t, ch] = got[64:96].astype(BF)
            via, away = (got[32:64], got[96:128]) if t < 2 else (got[96:128], got[32:64])
            keep[t, ch] = via
            sendd[t, ch] = away.astype(BF)
        forward, back = (up, down) if t < 2 else (down, up)
        first[t] = remote(send2.at[t], r1.at[t], m1_send.at[t], m1_recv.at[t], forward)
        direct[t] = remote(sendd.at[t], r3.at[:, :, cols], m3_send.at[t], m3_recv.at[t], back)
        done[t] = pltpu.make_async_copy(own.at[t], out.at[:, :, cols], own_sem.at[t])
        done[t].start()
        if i == 3:
            pass_on(order[0])
    for t in order[1:]:
        pass_on(t)
    for t in order:
        done[t].wait()
        direct[t].wait_recv()
        second[t].wait_recv()
    for t in order:
        first[t].wait_send()
        direct[t].wait_send()
        second[t].wait_send()


def solution(mesh):
    n_strip, n_lvl = mesh.shape["strip"], mesh.shape["lvl"]
    table = constants()

    def per_device(photos, seams, offsets):
        far = pl.BlockSpec(memory_space=pltpu.HBM)
        given = [jnp.asarray(table[name]) for name in NAMES]
        dma = pltpu.SemaphoreType.DMA
        tile = (4, 3, 32, 256)
        strip = (3, 32, N)
        out, r2, r3 = pl.pallas_call(
            functools.partial(kernel, n_strip, n_lvl),
            out_shape=(jax.ShapeDtypeStruct(strip, F32), jax.ShapeDtypeStruct(strip, BF), jax.ShapeDtypeStruct(strip, BF)),
            in_specs=[far] * (3 + len(NAMES)),
            out_specs=(far, far, far),
            scratch_shapes=[
                *[pltpu.VMEM(a.shape[1:] if name == "h35" else a.shape, a.dtype) for name, a in zip(NAMES, given)],
                dma((len(NAMES) + 5,)),
                pltpu.VMEM((4, 3, 64, N), BF),
                pltpu.SMEM((4,), jnp.int32),
                pltpu.VMEM((4, 2, 64), jnp.int32),
                pltpu.VMEM((256, 128), F32),
                pltpu.VMEM((256, 128), F32),
                pltpu.VMEM((4, 128, 1280), BF),
                pltpu.VMEM((512, 640), BF),
                pltpu.VMEM((512, 640), BF),
                pltpu.VMEM((512, 384), BF),
                pltpu.VMEM((3, 256, N), BF),
                pltpu.VMEM((192, 640), BF),
                pltpu.VMEM((192, 640), BF),
                pltpu.VMEM(tile, BF),
                pltpu.VMEM(tile, BF),
                pltpu.VMEM(tile, F32),
                pltpu.VMEM(tile, BF),
                pltpu.VMEM(tile, BF),
                pltpu.VMEM(tile, F32),
                dma((4,)),
                dma((2,)), dma((2,)), dma((4,)), dma((4,)), dma((4,)), dma((4,)), dma((4,)), dma((4,)),
            ],
            compiler_params=pltpu.CompilerParams(collective_id=0, has_side_effects=True),
        )(offsets, photos, seams, *given)
        return out + (r2.astype(F32) + r3.astype(F32))

    placed = (P("strip", None, None, "lvl"), P("strip", None, None), P("strip"))
    return jax.shard_map(
        per_device, mesh=mesh, in_specs=placed, out_specs=P(None, "strip", "lvl"), check_vma=False
    )
```

```python
import functools

import jax
import jax.numpy as jnp
import ml_dtypes
import numpy as np
from jax import lax
from jax.experimental import pallas as pl
from jax.experimental.pallas import tpu as pltpu
from jax.sharding import PartitionSpec as P

BF = jnp.bfloat16
F32 = jnp.float32
MESH = pl.DeviceIdType.MESH
TAPS = (0.0625, 0.25, 0.375, 0.25, 0.0625)
N = 1024
HALO = 128
WIDE = {0: 1280, 1: 640, 2: 320, 3: 160, 4: 80, 5: 40}
PAD = {1: 640, 2: 384, 3: 256, 4: 128, 5: 128}
ROWS = {0: 64, 1: 32, 2: 16, 3: 8, 4: 4, 5: 2}
SLOT = {2: (0, 64), 3: (64, 32), 4: (96, 16), 5: (112, 16)}


def reduce_rows(tall):
    m = np.zeros((tall // 2, tall))
    for i in range(tall // 2):
        for t in range(5):
            r = 2 * i + t - 2
            if 0 <= r < tall:
                m[i, r] = TAPS[t]
    return m


def expand_rows(tall):
    m = np.zeros((2 * tall, tall))
    for i in range(tall):
        for r, w in ((i - 1, 0.125), (i, 0.75), (i + 1, 0.125)):
            if 0 <= r < tall:
                m[2 * i, r] = w
        for r in (i, i + 1):
            if r < tall:
                m[2 * i + 1, r] = 0.5
    return m


def blocks(m, count):
    return np.kron(np.eye(count), m)


def bf(x):
    return np.asarray(x, np.float32).astype(ml_dtypes.bfloat16)


def split(x):
    hi = bf(x)
    return hi, bf(np.asarray(x, np.float64) - hi.astype(np.float64))


def valid(level, edge):
    e = np.arange(WIDE[level])
    h = HALO >> level
    n = N >> level
    keep = np.ones(WIDE[level])
    if edge == 0:
        keep[e < h] = 0
    if edge == 2:
        keep[e >= h + n] = 0
    return keep


def reduce_cols(level, edge):
    m = reduce_rows(WIDE[level]).T
    return m * valid(level + 1, edge)[None, :]


def constants():
    c = {}
    c["v1"] = bf(blocks(reduce_rows(64), 4))
    w = np.zeros((512, 128))
    for col in range(128):
        for t in range(5):
            w[128 + 2 * col + t - 2, col] = TAPS[t]
    c["wred"] = bf(w)
    v = {1: np.eye(32)}
    for k in (2, 3, 4, 5):
        v[k] = reduce_rows(ROWS[k - 1]) @ v[k - 1]
    v25 = np.zeros((128, 128))
    for k in (2, 3, 4, 5):
        start, _ = SLOT[k]
        v25[start : start + 4 * ROWS[k]] = blocks(v[k], 4)
    c["v25"] = bf(v25)
    h35 = np.zeros((3, 384, 384))
    for edge in range(3):
        m3 = reduce_cols(2, edge)
        m4 = m3 @ reduce_cols(3, edge)
        m5 = m4 @ reduce_cols(4, edge)
        h35[edge, :320, 0:160] = m3
        h35[edge, :320, 256:336] = m4
        h35[edge, :320, 336:376] = m5
    c["h35"] = bf(h35)
    c["er1"] = bf(blocks(expand_rows(16), 12))
    c["er2"] = bf(blocks(expand_rows(8), 12))
    c["er3"] = bf(blocks(expand_rows(4), 12))
    er4 = np.zeros((48, 48))
    for ch in range(3):
        er4[16 * ch : 16 * ch + 16, 16 * ch : 16 * ch + 8] = blocks(expand_rows(2), 4)
    c["er4"] = bf(er4)
    for k in (1, 2, 3, 4):
        m = np.zeros((PAD[k + 1], PAD[k]))
        at = 80 if k == 4 else 0
        m[at : at + WIDE[k + 1], : WIDE[k]] = expand_rows(WIDE[k + 1]).T
        if k == 1:
            c["ec1a"], c["ec1b"] = bf(m[0:256, 0:384]), bf(m[128:384, 384:640])
        else:
            c[f"ec{k}"] = bf(m)
    e0 = np.zeros((256, 256))
    for col in range(256):
        i = 64 + col // 2
        if col % 2 == 0:
            e0[i - 1, col], e0[i, col], e0[i + 1, col] = 0.125, 0.75, 0.125
        else:
            e0[i, col], e0[i + 1, col] = 0.5, 0.5
    c["e0"] = bf(e0)
    er0 = blocks(expand_rows(32), 4)
    one = expand_rows(18)[2:34]
    tall = np.zeros((96, 64))
    for ch in range(3):
        tall[32 * ch : 32 * ch + 32, 18 * ch : 18 * ch + 18] = one
    c["tall"] = bf(np.concatenate([tall, tall], axis=1))
    c["d0"] = bf(np.concatenate([er0, er0], axis=1))
    hi = np.zeros((3, 64, 640))
    lo = np.zeros((3, 64, 640))
    for first in range(3):
        up = np.eye(64)
        for k in (1, 2, 3, 4, 5):
            h = 32 >> k
            if k > 1:
                up = up @ expand_rows(4 * h)
            place = np.zeros((4 * h, 2 * h))
            place[first * h : first * h + 2 * h] = np.eye(2 * h)
            m = np.tile(up @ place, (1, 4))
            a, b = split(m)
            s = 128 * (k - 1)
            hi[first, :, s : s + m.shape[1]] = a.astype(np.float64)
            lo[first, :, s : s + m.shape[1]] = b.astype(np.float64)
    c["lb"] = bf(hi)
    c["lb5"] = bf(lo[:, :, 384:])
    assert not lo[:, :, :384].any()
    pm = np.full((8, 640), -1.0)
    for k in (1, 2, 3, 4, 5):
        for p in range(4):
            s = 128 * (k - 1) + p * ROWS[k]
            pm[:, s : s + ROWS[k]] = p
    c["pm"] = pm.astype(np.float32)
    return c


NAMES = ("v1", "wred", "v25", "h35", "er1", "er2", "er3", "er4", "ec1a", "ec1b", "ec2", "ec3", "ec4", "e0", "d0", "lb", "lb5", "pm")


def dot(a, b):
    return jnp.dot(a, b, preferred_element_type=F32)


def halves(x):
    hi = x.astype(BF)
    return hi, (x - hi.astype(F32)).astype(BF)


def kernel(n_strip, n_lvl, offsets_in, photos_in, seams_in, *refs):
    n = len(NAMES)
    given, outs, held, rest = refs[:n], refs[n : n + 5], refs[n + 5 : 2 * n + 5], refs[2 * n + 5 :]
    body(n_strip, n_lvl, offsets_in, photos_in, seams_in, dict(zip(NAMES, given)), *outs, dict(zip(NAMES, held)), *rest)


def body(n_strip, n_lvl, offsets_in, photos_in, seams_in, given, base_out, own_out, q1, q2, q3, held, load, photos, offsets, seams, s0, s1, tm, g1,
         ys, y2, uh, ul, sent, got_in, base, low, lowo, out_sem,
         halo_send, halo_recv, m_send, m_recv, n_send, n_recv):
    x = lax.axis_index("strip")
    me = lax.axis_index("lvl")
    right, left = lax.rem(me + 1, n_lvl), lax.rem(me + n_lvl - 1, n_lvl)
    others = [lax.rem(x + j, n_strip) for j in range(n_strip)]
    barrier = pltpu.get_barrier_semaphore()
    for target in ({"lvl": left}, {"lvl": right}, {"strip": others[1]}, {"strip": others[2]}, {"strip": others[3]}):
        pl.semaphore_signal(barrier, inc=1, device_id=target, device_id_type=MESH)
    edge = jnp.where(me == 0, 0, jnp.where(me == n_lvl - 1, 2, 1))
    waits = {}

    def fetch(name, src, dst):
        copy = pltpu.make_async_copy(src, dst, load.at[len(waits)])
        copy.start()
        waits[name] = copy

    def ready(name):
        if waits[name] is not None:
            waits[name].wait()
            waits[name] = None

    def const(name):
        ready(name)
        return held[name]

    fetch("seams", seams_in, seams)
    fetch("v1", given["v1"], held["v1"])
    for ch in range(3):
        fetch(ch, photos_in.at[:, ch], photos.at[:, ch])
    fetch("offsets", offsets_in, offsets)
    for name in NAMES[1:]:
        fetch(name, given[name].at[edge] if name == "h35" else given[name], held[name])

    def rows_of(ch, start, width):
        return photos[:, ch, :, start : start + width].reshape(256, width)

    lead = const("v1")[...]
    for ch in range(3):
        ready(ch)
    for start in (0, N - 128):
        for ch in range(3):
            tm[ch, :, HALO + start : HALO + start + 128] = dot(lead, rows_of(ch, start, 128)).astype(BF)
    pl.semaphore_wait(barrier, 5)
    halo = []
    for i, (src, dst, target) in enumerate(((HALO, HALO + N, left), (N, 0, right))):
        copy = pltpu.make_async_remote_copy(
            src_ref=tm.at[0:3, :, src : src + 128],
            dst_ref=tm.at[0:3, :, dst : dst + 128],
            send_sem=halo_send.at[i],
            recv_sem=halo_recv.at[i],
            device_id={"lvl": target},
            device_id_type=MESH,
        )
        copy.start()
        halo.append(copy)
    r_i = lax.broadcasted_iota(jnp.int32, (64, 64), 0)
    c_i = lax.broadcasted_iota(jnp.int32, (64, 64), 1)
    eye = r_i == c_i
    ready("seams")
    for p in range(4):
        for e, dst in ((0, s0), (1, s1)):
            line = seams[p, e : e + 1, :].astype(F32)
            col = jnp.sum(jnp.where(eye, line, 0.0), axis=1, keepdims=True)
            dst[64 * p : 64 * p + 64, :] = jnp.broadcast_to(col, (64, 128))

    first_col = (me * N).astype(F32)

    def mask_tile(start):
        col = lax.broadcasted_iota(jnp.int32, (256, 128), 1).astype(F32) + (first_col + (start - HALO))
        a, b = s0[...], s1[...]
        return jnp.concatenate([(c >= a) & (c < b) for c in (col, col + 128.0)], axis=1)

    for ch in range(3):
        tm[ch, :, 256 : N] = dot(lead, rows_of(ch, 128, N - 256)).astype(BF)
    for start in range(0, N + 256, 256):
        m = jnp.where(mask_tile(start), 1.0, 0.0).astype(BF)
        tm[3, :, start : start + 256] = dot(lead, m).astype(BF)

    wred = const("wred")

    def g1_tile(j):
        a, b = max(0, 2 * j - 1), min(10, 2 * j + 3)
        w = wred[128 * (a - 2 * j + 1) : 128 * (b - 2 * j + 1), :]
        val = dot(tm[:, :, 128 * a : 128 * b].reshape(512, 128 * (b - a)), w)
        if j in (0, 4):
            col = lax.broadcasted_iota(jnp.int32, (1, 128), 1) + (128 * j - 64) + me * (N // 2)
            val = jnp.where((col >= 0) & (col < n_lvl * (N // 2)), val, 0.0)
        g1[:, 128 * j : 128 * j + 128] = val.astype(BF)

    for j in (1, 2, 3):
        g1_tile(j)
    e0, d0 = const("e0"), const("d0")
    ready("offsets")
    places = [offsets[p] for p in range(4)]

    q = lax.broadcasted_iota(jnp.int32, (128, 256), 0)
    lane = lax.broadcasted_iota(jnp.int32, (128, 256), 1)
    where = jnp.where(lane < 64, places[0], jnp.where(lane < 128, places[1], jnp.where(lane < 192, places[2], places[3])))
    put = jnp.where((((q >> 5) + x) & 3) * 32 + (q & 31) == where * 32 + (lane & 63), 1.0, 0.0).astype(BF)

    def remote(src, dst, send, recv, target):
        copy = pltpu.make_async_remote_copy(
            src_ref=src, dst_ref=dst, send_sem=send, recv_sem=recv, device_id={"strip": target}, device_id_type=MESH
        )
        copy.start()
        return copy

    sends = []

    def widened(t):
        hi, lo = halves(dot(g1[0:384, 128 * t : 128 * t + 256], e0[...]))
        uh[t], ul[t] = hi, lo

    def band(t, ch):
        r = slice(128 * ch, 128 * ch + 128)
        away = dot(d0[...], jnp.concatenate([uh[t, r], ul[t, r]], axis=0))
        detail = rows_of(ch, 256 * t, 256).astype(F32) - away
        weighted_0 = jnp.where(mask_tile(HALO + 256 * t), detail, 0.0).astype(BF)
        got = dot(put, weighted_0).astype(BF)
        for j in range(4):
            sent[t, j, ch] = got[32 * j : 32 * j + 32]

    def send_band(t):
        for j in (2, 1, 3):
            sends.append(remote(sent.at[t, j], got_in.at[t, j], m_send.at[t, j - 1], m_recv.at[t, j - 1], others[j]))

    widened(1)
    widened(2)
    for t in (1, 2):
        for ch in range(3):
            band(t, ch)
        send_band(t)
    for name in NAMES:
        ready(name)
    for copy in halo:
        copy.wait()
    for at, outer in ((0, 0), (N + 128, n_lvl - 1)):
        tm[0:3, :, at : at + 128] = jnp.where(me == outer, jnp.zeros((), BF), tm[0:3, :, at : at + 128])
    for j in (0, 4):
        g1_tile(j)
    widened(0)
    widened(3)

    for ch in range(4):
        ys[128 * ch : 128 * ch + 128, :] = dot(const("v25")[...], g1[128 * ch : 128 * ch + 128, :]).astype(BF)
    col = lax.broadcasted_iota(jnp.int32, (1, 384), 1) - 32 + me * (N // 4)
    inside = (col >= 0) & (col < n_lvl * (N // 4))
    for j, a, b in ((0, 0, 3), (1, 1, 5), (2, 3, 5)):
        w = wred[128 * (a - 2 * j + 1) : 128 * (b - 2 * j + 1), :]
        val = dot(ys[:, 128 * a : 128 * b], w)
        y2[:, 128 * j : 128 * j + 128] = jnp.where(inside[:, 128 * j : 128 * j + 128], val, 0.0).astype(BF)
    band(0, 0)
    y = y2[...].reshape(4, 128, 384)
    g2 = y[:, 0:64].reshape(256, 384)
    y35 = dot(y[:, 64:128].reshape(256, 384), const("h35")[...]).astype(BF).reshape(4, 64, 384)
    g3 = y35[:, 0:32, 0:256].reshape(128, 256)
    g4 = y35[:, 32:48, 256:384].reshape(64, 128)
    g5 = y35[:, 48:64, 256:384].reshape(64, 128)
    band(0, 1)
    gs = {1: g1[...], 2: g2, 3: g3, 4: g4, 5: g5}

    weighted = {}
    er = {k: const(f"er{k}") for k in (1, 2, 3, 4)}

    def widen(k, field):
        if k == 1:
            return jnp.concatenate([dot(field[:, 0:256], held["ec1a"][...]), dot(field[:, 128:384], held["ec1b"][...])], axis=1)
        return dot(field, held[f"ec{k}"][...])

    for k, color in ((4, 48), (3, 48), (2, 96), (1, 192)):
        tall = 4 * ROWS[k]
        u_hi, u_lo = halves(dot(er[k][...], gs[k + 1][0:color]))
        expanded = widen(k, jnp.concatenate([u_hi, u_lo], axis=0))
        half = 3 * tall
        g = gs[k].astype(F32)
        detail = g[0:half] - (expanded[0:half] + expanded[half:])
        m = g[half:]
        weighted[k] = [(m * detail[ch * tall : ch * tall + tall]).astype(BF) for ch in range(3)]
    band(0, 2)
    send_band(0)
    g = g5.astype(F32)
    weighted[5] = [(g[48:64] * g[16 * ch : 16 * ch + 16]).astype(BF) for ch in range(3)]

    pm, lb, lb5 = const("pm"), const("lb"), const("lb5")

    def by_photo(which):
        got = jnp.zeros(which.shape, F32)
        for p in range(4):
            got = jnp.where(which == float(p), places[p].astype(F32), got)
        return got

    spot = by_photo(pm[0:1, :])
    table = sum(jnp.where(spot == float(o), lb[o].astype(F32), 0.0) for o in range(3)).astype(BF)
    fine = sum(jnp.where(spot[:, 384:] == float(o), lb5[o].astype(F32), 0.0) for o in range(3)).astype(BF)
    band(3, 0)
    placed = {}
    for k in (5, 4, 3, 2, 1):
        s = 128 * (k - 1)
        size = {1: 128, 2: 64, 3: 32, 4: 16, 5: 16}[k]
        lhs = table[:, s : s + size]
        if k >= 4:
            lhs = jnp.concatenate([lhs, fine[:, s - 384 : s - 384 + size]], axis=0)
        parts = []
        for ch in range(3):
            got = dot(lhs, weighted[k][ch])
            parts.append(got[0:64] + got[64:128] if k >= 4 else got)
        placed[k] = jnp.concatenate(parts, axis=0)

    band(3, 1)
    total = placed[5]
    for k in (4, 3, 2, 1):
        hi, lo = halves(total)
        got = widen(k, jnp.concatenate([hi, lo], axis=0))
        col = lax.broadcasted_iota(jnp.int32, (1, PAD[k]), 1) - (HALO >> k) + me * (N >> k)
        ok = (col >= 0) & (col < n_lvl * (N >> k))
        total = placed[k] + jnp.where(ok, got[0:192] + got[192:384], 0.0)
        if k == 4:
            band(3, 2)
            send_band(3)
    q = lax.broadcasted_iota(jnp.int32, (256, 192), 0)
    k = lax.broadcasted_iota(jnp.int32, (256, 192), 1)
    rest = q & 63
    ch = jnp.where(rest >= 18, 1, 0) + jnp.where(rest >= 36, 1, 0)
    row = (((q >> 6) + x) & 3) * 16 + rest - 18 * ch - 1
    pick = jnp.where((rest < 54) & (row == (k & 63)) & (ch == (k >> 6)), 1.0, 0.0).astype(BF)
    hi, lo = halves(total)
    got = dot(pick, hi)
    lows = []
    for j, there in ((2, q2), (1, q1), (3, q3)):
        low[j - 1] = got[64 * j : 64 * j + 64].astype(BF)
        lows.append(remote(low.at[j - 1], there, n_send.at[j - 1], n_recv.at[j - 1], others[j]))
    lowo[...] = got[0:64] + dot(pick[0:64], lo)
    copies = [pltpu.make_async_copy(lowo, own_out, out_sem.at[0])]
    copies[0].start()

    for copy in sends:
        copy.wait_recv()
    for t in range(4):
        base[:, :, 256 * t : 256 * t + 256] = (sent[t, 0] + got_in[t, 1]) + (got_in[t, 2] + got_in[t, 3])
    copies.append(pltpu.make_async_copy(base, base_out, out_sem.at[1]))
    copies[1].start()
    for copy in sends:
        copy.wait_send()
    for copy in lows:
        copy.wait()
    for copy in copies:
        copy.wait()


def finish(base, low, q1, q2, q3, e0, tall, out):
    total = low[...] + (q2[...].astype(F32) + (q1[...].astype(F32) + q3[...].astype(F32)))
    hi, lo = halves(total)
    hi, lo = halves(dot(tall[...], jnp.concatenate([hi, lo], axis=0)))
    for t in range(4):
        cols = slice(128 * t, 128 * t + 256)
        got = dot(jnp.concatenate([hi[:, cols], lo[:, cols]], axis=0), e0[...])
        cols = slice(256 * t, 256 * t + 256)
        out[:, :, cols] = base[:, :, cols].astype(F32) + (got[0:96] + got[96:192]).reshape(3, 32, 256)


def solution(mesh):
    n_strip, n_lvl = mesh.shape["strip"], mesh.shape["lvl"]
    table = constants()

    def per_device(photos, seams, offsets):
        far = pl.BlockSpec(memory_space=pltpu.HBM)
        given = [jnp.asarray(table[name]) for name in NAMES]
        dma = pltpu.SemaphoreType.DMA
        tile = (4, 3, 32, 256)
        strip = (3, 32, N)
        low_shape = jax.ShapeDtypeStruct((64, 640), BF)
        base, low, *rest = pl.pallas_call(
            functools.partial(kernel, n_strip, n_lvl),
            out_shape=(
                jax.ShapeDtypeStruct(strip, BF),
                jax.ShapeDtypeStruct((64, 640), F32),
                low_shape,
                low_shape,
                low_shape,
            ),
            in_specs=[far] * (3 + len(NAMES)),
            out_specs=(far,) * 5,
            scratch_shapes=[
                *[pltpu.VMEM(a.shape[1:] if name == "h35" else a.shape, a.dtype) for name, a in zip(NAMES, given)],
                dma((len(NAMES) + 5,)),
                pltpu.VMEM((4, 3, 64, N), BF),
                pltpu.SMEM((4,), jnp.int32),
                pltpu.VMEM((4, 2, 64), jnp.int32),
                pltpu.VMEM((256, 128), F32),
                pltpu.VMEM((256, 128), F32),
                pltpu.VMEM((4, 128, 1280), BF),
                pltpu.VMEM((512, 640), BF),
                pltpu.VMEM((512, 640), BF),
                pltpu.VMEM((512, 384), BF),
                pltpu.VMEM((4, 384, 256), BF),
                pltpu.VMEM((4, 384, 256), BF),
                pltpu.VMEM((4, *tile), BF),
                pltpu.VMEM((4, *tile), BF),
                pltpu.VMEM(strip, BF),
                pltpu.VMEM((3, 64, 640), BF),
                pltpu.VMEM((64, 640), F32),
                *[dma((2,))] * 3,
                dma((4, 3)), dma((4, 3)), dma((3,)), dma((3,)),
            ],
            compiler_params=pltpu.CompilerParams(collective_id=0, has_side_effects=True),
        )(offsets, photos, seams, *given)
        near = pl.BlockSpec(memory_space=pltpu.VMEM)
        return pl.pallas_call(
            finish, out_shape=jax.ShapeDtypeStruct(strip, F32), in_specs=[near] * 7, out_specs=near
        )(base, low, *rest, jnp.asarray(table["e0"]), jnp.asarray(table["tall"]))

    placed = (P("strip", None, None, "lvl"), P("strip", None, None), P("strip"))
    return jax.shard_map(
        per_device, mesh=mesh, in_specs=placed, out_specs=P(None, "strip", "lvl"), check_vma=False
    )
```

```python
import functools

import jax
import jax.numpy as jnp
import ml_dtypes
import numpy as np
from jax import lax
from jax.experimental import pallas as pl
from jax.experimental.pallas import tpu as pltpu
from jax.sharding import PartitionSpec as P

BF = jnp.bfloat16
F32 = jnp.float32
MESH = pl.DeviceIdType.MESH
TAPS = (0.0625, 0.25, 0.375, 0.25, 0.0625)
N = 1024
HALO = 128
WIDE = {0: 1280, 1: 640, 2: 320, 3: 160, 4: 80, 5: 40}
PAD = {1: 640, 2: 384, 3: 256, 4: 128, 5: 128}
ROWS = {0: 64, 1: 32, 2: 16, 3: 8, 4: 4, 5: 2}
SLOT = {2: (0, 64), 3: (64, 32), 4: (96, 16), 5: (112, 16)}


def reduce_rows(tall):
    m = np.zeros((tall // 2, tall))
    for i in range(tall // 2):
        for t in range(5):
            r = 2 * i + t - 2
            if 0 <= r < tall:
                m[i, r] = TAPS[t]
    return m


def expand_rows(tall):
    m = np.zeros((2 * tall, tall))
    for i in range(tall):
        for r, w in ((i - 1, 0.125), (i, 0.75), (i + 1, 0.125)):
            if 0 <= r < tall:
                m[2 * i, r] = w
        for r in (i, i + 1):
            if r < tall:
                m[2 * i + 1, r] = 0.5
    return m


def blocks(m, count):
    return np.kron(np.eye(count), m)


def bf(x):
    return np.asarray(x, np.float32).astype(ml_dtypes.bfloat16)


def split(x):
    hi = bf(x)
    return hi, bf(np.asarray(x, np.float64) - hi.astype(np.float64))


def valid(level, edge):
    e = np.arange(WIDE[level])
    h = HALO >> level
    n = N >> level
    keep = np.ones(WIDE[level])
    if edge == 0:
        keep[e < h] = 0
    if edge == 2:
        keep[e >= h + n] = 0
    return keep


def reduce_cols(level, edge):
    m = reduce_rows(WIDE[level]).T
    return m * valid(level + 1, edge)[None, :]


def constants():
    c = {}
    c["v1"] = bf(blocks(reduce_rows(64), 4))
    w = np.zeros((512, 128))
    for col in range(128):
        for t in range(5):
            w[128 + 2 * col + t - 2, col] = TAPS[t]
    c["wred"] = bf(w)
    v = {1: np.eye(32)}
    for k in (2, 3, 4, 5):
        v[k] = reduce_rows(ROWS[k - 1]) @ v[k - 1]
    v25 = np.zeros((128, 128))
    for k in (2, 3, 4, 5):
        start, _ = SLOT[k]
        v25[start : start + 4 * ROWS[k]] = blocks(v[k], 4)
    c["v25"] = bf(v25)
    h35 = np.zeros((3, 384, 384))
    for edge in range(3):
        m3 = reduce_cols(2, edge)
        m4 = m3 @ reduce_cols(3, edge)
        m5 = m4 @ reduce_cols(4, edge)
        h35[edge, :320, 0:160] = m3
        h35[edge, :320, 256:336] = m4
        h35[edge, :320, 336:376] = m5
    c["h35"] = bf(h35)
    c["er1"] = bf(blocks(expand_rows(16), 12))
    c["er2"] = bf(blocks(expand_rows(8), 12))
    c["er3"] = bf(blocks(expand_rows(4), 12))
    er4 = np.zeros((48, 48))
    for ch in range(3):
        er4[16 * ch : 16 * ch + 16, 16 * ch : 16 * ch + 8] = blocks(expand_rows(2), 4)
    c["er4"] = bf(er4)
    for k in (1, 2, 3, 4):
        m = np.zeros((PAD[k + 1], PAD[k]))
        at = 80 if k == 4 else 0
        m[at : at + WIDE[k + 1], : WIDE[k]] = expand_rows(WIDE[k + 1]).T
        if k == 1:
            c["ec1a"], c["ec1b"] = bf(m[0:256, 0:384]), bf(m[128:384, 384:640])
        else:
            c[f"ec{k}"] = bf(m)
    e0 = np.zeros((256, 256))
    for col in range(256):
        i = 64 + col // 2
        if col % 2 == 0:
            e0[i - 1, col], e0[i, col], e0[i + 1, col] = 0.125, 0.75, 0.125
        else:
            e0[i, col], e0[i + 1, col] = 0.5, 0.5
    c["e0"] = bf(e0)
    er0 = blocks(expand_rows(32), 4)
    one = expand_rows(18)[2:34]
    tall = np.zeros((96, 64))
    for ch in range(3):
        tall[32 * ch : 32 * ch + 32, 18 * ch : 18 * ch + 18] = one
    c["tall"] = bf(np.concatenate([tall, tall], axis=1))
    c["d0"] = bf(np.concatenate([er0, er0], axis=1))
    hi = np.zeros((3, 64, 640))
    lo = np.zeros((3, 64, 640))
    for first in range(3):
        up = np.eye(64)
        for k in (1, 2, 3, 4, 5):
            h = 32 >> k
            if k > 1:
                up = up @ expand_rows(4 * h)
            place = np.zeros((4 * h, 2 * h))
            place[first * h : first * h + 2 * h] = np.eye(2 * h)
            m = np.tile(up @ place, (1, 4))
            a, b = split(m)
            s = 128 * (k - 1)
            hi[first, :, s : s + m.shape[1]] = a.astype(np.float64)
            lo[first, :, s : s + m.shape[1]] = b.astype(np.float64)
    c["lb"] = bf(hi)
    c["lb5"] = bf(lo[:, :, 384:])
    assert not lo[:, :, :384].any()
    pm = np.full((8, 640), -1.0)
    for k in (1, 2, 3, 4, 5):
        for p in range(4):
            s = 128 * (k - 1) + p * ROWS[k]
            pm[:, s : s + ROWS[k]] = p
    c["pm"] = pm.astype(np.float32)
    return c


NAMES = ("v1", "wred", "v25", "h35", "er1", "er2", "er3", "er4", "ec1a", "ec1b", "ec2", "ec3", "ec4", "e0", "d0", "lb", "lb5", "pm")


def dot(a, b):
    return jnp.dot(a, b, preferred_element_type=F32)


def halves(x):
    hi = x.astype(BF)
    return hi, (x - hi.astype(F32)).astype(BF)


def kernel(n_strip, n_lvl, offsets_in, photos_in, seams_in, *refs):
    n = len(NAMES)
    given, outs, held, rest = refs[:n], refs[n : n + 9], refs[n + 9 : 2 * n + 9], refs[2 * n + 9 :]
    body(n_strip, n_lvl, offsets_in, photos_in, seams_in, dict(zip(NAMES, given)), *outs, dict(zip(NAMES, held)), *rest)


def body(n_strip, n_lvl, offsets_in, photos_in, seams_in, given, base_out, own_out, late_out, q1, q2, q3, l1, l2, l3, held, load, photos, offsets, seams, s0, s1, tm, g1,
         ys, y2, mk, uh, ul, sent, got_in, base, low, lowo, kept, late, lateo, out_sem,
         halo_send, halo_recv, m_send, m_recv, n_send, n_recv, p_send, p_recv):
    x = lax.axis_index("strip")
    me = lax.axis_index("lvl")
    right, left = lax.rem(me + 1, n_lvl), lax.rem(me + n_lvl - 1, n_lvl)
    others = [lax.rem(x + j, n_strip) for j in range(n_strip)]
    barrier = pltpu.get_barrier_semaphore()
    for target in ({"lvl": left}, {"lvl": right}, {"strip": others[1]}, {"strip": others[2]}, {"strip": others[3]}):
        pl.semaphore_signal(barrier, inc=1, device_id=target, device_id_type=MESH)
    edge = jnp.where(me == 0, 0, jnp.where(me == n_lvl - 1, 2, 1))
    waits = {}

    def fetch(name, src, dst):
        copy = pltpu.make_async_copy(src, dst, load.at[len(waits)])
        copy.start()
        waits[name] = copy

    def ready(name):
        if waits[name] is not None:
            waits[name].wait()
            waits[name] = None

    def const(name):
        ready(name)
        return held[name]

    fetch("seams", seams_in, seams)
    fetch("v1", given["v1"], held["v1"])
    for name, at, width in (("west", 0, 128), ("east", N - 128, 128), ("middle", 128, N - 256)):
        cols = slice(at, at + width)
        fetch(name, photos_in.at[:, :, :, cols], photos.at[:, :, :, cols])
    fetch("offsets", offsets_in, offsets)
    for name in NAMES[1:]:
        fetch(name, given[name].at[edge] if name == "h35" else given[name], held[name])

    def rows_of(ch, start, width):
        return photos[:, ch, :, start : start + width].reshape(256, width)

    lead = const("v1")[...]
    ready("west")
    ready("east")
    for start in (0, N - 128):
        for ch in range(3):
            tm[ch, :, HALO + start : HALO + start + 128] = dot(lead, rows_of(ch, start, 128)).astype(BF)
    pl.semaphore_wait(barrier, 5)
    halo = []
    for i, (src, dst, target) in enumerate(((HALO, HALO + N, left), (N, 0, right))):
        copy = pltpu.make_async_remote_copy(
            src_ref=tm.at[0:3, :, src : src + 128],
            dst_ref=tm.at[0:3, :, dst : dst + 128],
            send_sem=halo_send.at[i],
            recv_sem=halo_recv.at[i],
            device_id={"lvl": target},
            device_id_type=MESH,
        )
        copy.start()
        halo.append(copy)
    r_i = lax.broadcasted_iota(jnp.int32, (64, 64), 0)
    c_i = lax.broadcasted_iota(jnp.int32, (64, 64), 1)
    eye = r_i == c_i
    ready("seams")
    for p in range(4):
        for e, dst in ((0, s0), (1, s1)):
            line = seams[p, e : e + 1, :].astype(F32)
            col = jnp.sum(jnp.where(eye, line, 0.0), axis=1, keepdims=True)
            dst[64 * p : 64 * p + 64, :] = jnp.broadcast_to(col, (64, 128))

    first_col = (me * N).astype(F32)

    def mask_tile(start):
        col = lax.broadcasted_iota(jnp.int32, (256, 128), 1).astype(F32) + (first_col + (start - HALO))
        a, b = s0[...], s1[...]
        return jnp.concatenate([(c >= a) & (c < b) for c in (col, col + 128.0)], axis=1)

    for start in range(0, N + 256, 256):
        m = jnp.where(mask_tile(start), 1.0, 0.0).astype(BF)
        mk[:, start : start + 256] = m
        tm[3, :, start : start + 256] = dot(lead, m).astype(BF)
    ready("middle")
    for ch in range(3):
        tm[ch, :, 256 : N] = dot(lead, rows_of(ch, 128, N - 256)).astype(BF)

    wred = const("wred")

    def g1_tile(j, lo=0, hi=4):
        a, b = max(0, 2 * j - 1), min(10, 2 * j + 3)
        w = wred[128 * (a - 2 * j + 1) : 128 * (b - 2 * j + 1), :]
        val = dot(tm[lo:hi, :, 128 * a : 128 * b].reshape(128 * (hi - lo), 128 * (b - a)), w)
        if j in (0, 4):
            col = lax.broadcasted_iota(jnp.int32, (1, 128), 1) + (128 * j - 64) + me * (N // 2)
            val = jnp.where((col >= 0) & (col < n_lvl * (N // 2)), val, 0.0)
        g1[128 * lo : 128 * hi, 128 * j : 128 * j + 128] = val.astype(BF)

    for j in (1, 2):
        g1_tile(j)
    e0, d0 = const("e0"), const("d0")
    ready("offsets")
    places = [offsets[p] for p in range(4)]

    q = lax.broadcasted_iota(jnp.int32, (128, 256), 0)
    lane = lax.broadcasted_iota(jnp.int32, (128, 256), 1)
    where = jnp.where(lane < 64, places[0], jnp.where(lane < 128, places[1], jnp.where(lane < 192, places[2], places[3])))
    put = jnp.where((((q >> 5) + x) & 3) * 32 + (q & 31) == where * 32 + (lane & 63), 1.0, 0.0).astype(BF)

    def remote(src, dst, send, recv, target):
        copy = pltpu.make_async_remote_copy(
            src_ref=src, dst_ref=dst, send_sem=send, recv_sem=recv, device_id={"strip": target}, device_id_type=MESH
        )
        copy.start()
        return copy

    sends = []

    def widened(t):
        hi, lo = halves(dot(g1[0:384, 128 * t : 128 * t + 256], e0[...]))
        uh[t], ul[t] = hi, lo

    def band(t, ch):
        r = slice(128 * ch, 128 * ch + 128)
        away = dot(d0[...], jnp.concatenate([uh[t, r], ul[t, r]], axis=0))
        detail = rows_of(ch, 256 * t, 256).astype(F32) - away
        weighted_0 = detail.astype(BF) * mk[:, HALO + 256 * t : HALO + 256 * t + 256]
        if t in (0, 3):
            kept[t // 3, ch] = weighted_0
            return
        got = dot(put, weighted_0).astype(BF)
        for j in range(4):
            sent[t - 1, j, ch] = got[32 * j : 32 * j + 32]

    def send_band(t):
        for j in (2, 1, 3):
            k = j - 1
            sends.append(remote(sent.at[t - 1, j], got_in.at[t - 1, j], m_send.at[t - 1, k], m_recv.at[t - 1, k], others[j]))

    for t in (1, 2):
        if t == 2:
            g1_tile(3)
        widened(t)
        for ch in range(3):
            band(t, ch)
        send_band(t)
    for name in NAMES:
        ready(name)
    col2 = lax.broadcasted_iota(jnp.int32, (1, 384), 1) - 32 + me * (N // 4)
    inside2 = (col2 >= 0) & (col2 < n_lvl * (N // 4))

    def deep(lo, hi):
        count = hi - lo
        rows = slice(128 * lo, 128 * hi)
        for ch in range(lo, hi):
            ys[128 * ch : 128 * ch + 128, :] = dot(held["v25"][...], g1[128 * ch : 128 * ch + 128, :]).astype(BF)
        for j, a, b in ((0, 0, 3), (1, 1, 5), (2, 3, 5)):
            w = wred[128 * (a - 2 * j + 1) : 128 * (b - 2 * j + 1), :]
            val = dot(ys[rows, 128 * a : 128 * b], w)
            y2[rows, 128 * j : 128 * j + 128] = jnp.where(inside2[:, 128 * j : 128 * j + 128], val, 0.0).astype(BF)
        y = y2[rows, :].reshape(count, 128, 384)
        y35 = dot(y[:, 64:128].reshape(64 * count, 384), held["h35"][...]).astype(BF).reshape(count, 64, 384)
        return {
            1: g1[rows, :],
            2: y[:, 0:64].reshape(64 * count, 384),
            3: y35[:, 0:32, 0:256].reshape(32 * count, 256),
            4: y35[:, 32:48, 256:384].reshape(16 * count, 128),
            5: y35[:, 48:64, 256:384].reshape(16 * count, 128),
        }

    for j in (0, 4):
        g1_tile(j, 3, 4)
    ms = deep(3, 4)

    pm, lb, lb5 = held["pm"], held["lb"], held["lb5"]

    def by_photo(which):
        got = jnp.zeros(which.shape, F32)
        for p in range(4):
            got = jnp.where(which == float(p), places[p].astype(F32), got)
        return got

    spot = by_photo(pm[0:1, :])
    table = sum(jnp.where(spot == float(o), lb[o].astype(F32), 0.0) for o in range(3)).astype(BF)
    fine = sum(jnp.where(spot[:, 384:] == float(o), lb5[o].astype(F32), 0.0) for o in range(3)).astype(BF)
    q = lax.broadcasted_iota(jnp.int32, (128, 128), 0)
    row = (((q >> 5) + x) & 3) * 32 + (q & 31)
    d = (lax.broadcasted_iota(jnp.int32, (128, 128), 1) & 63) - (row >> 1)
    even = jnp.where(d == 0, 0.75, jnp.where((d == 1) | (d == -1), 0.125, 0.0))
    odd = jnp.where((d == 0) | (d == 1), 0.5, 0.0)
    last = jnp.concatenate([put, jnp.where((row & 1) == 0, even, odd).astype(BF)], axis=1)

    q = lax.broadcasted_iota(jnp.int32, (256, 192), 0)
    k = lax.broadcasted_iota(jnp.int32, (256, 192), 1)
    rest = q & 63
    chan = jnp.where(rest >= 18, 1, 0) + jnp.where(rest >= 36, 1, 0)
    row = (((q >> 6) + x) & 3) * 16 + rest - 18 * chan - 1
    pick = jnp.where((rest < 54) & (row == (k & 63)) & (chan == (k >> 6)), 1.0, 0.0).astype(BF)
    for copy in halo:
        copy.wait()
    for at, outer in ((0, 0), (N + 128, n_lvl - 1)):
        tm[0:3, :, at : at + 128] = jnp.where(me == outer, jnp.zeros((), BF), tm[0:3, :, at : at + 128])
    for t in (0, 3):
        g1_tile(0 if t == 0 else 4, 0, 3)
        widened(t)

    gs = deep(0, 3)
    band(0, 0)
    band(0, 1)

    weighted = {}
    er = {k: const(f"er{k}") for k in (1, 2, 3, 4)}

    def widen(k, field):
        if k == 1:
            return jnp.concatenate([dot(field[:, 0:256], held["ec1a"][...]), dot(field[:, 128:384], held["ec1b"][...])], axis=1)
        return dot(field, held[f"ec{k}"][...])

    for k, color in ((4, 48), (3, 48), (2, 96), (1, 192)):
        tall = 4 * ROWS[k]
        rough = dot(er[k][...], gs[k + 1][0:color])
        expanded = widen(k, jnp.concatenate(halves(rough), axis=0))
        expanded = expanded[: 3 * tall] + expanded[3 * tall :]
        m = ms[k].astype(F32)
        detail = gs[k].astype(F32) - expanded
        weighted[k] = [(m * detail[ch * tall : ch * tall + tall]).astype(BF) for ch in range(3)]
    weighted[5] = [(ms[5].astype(F32) * gs[5][16 * ch : 16 * ch + 16].astype(F32)).astype(BF) for ch in range(3)]

    band(0, 2)
    band(3, 0)
    placed = {}
    for k in (5, 4, 3, 2, 1):
        s = 128 * (k - 1)
        size = {1: 128, 2: 64, 3: 32, 4: 16, 5: 16}[k]
        lhs = table[:, s : s + size]
        if k >= 4:
            lhs = jnp.concatenate([lhs, fine[:, s - 384 : s - 384 + size]], axis=0)
        parts = []
        for ch in range(3):
            got = dot(lhs, weighted[k][ch])
            parts.append(got[0:64] + got[64:128] if k >= 4 else got)
        placed[k] = jnp.concatenate(parts, axis=0)

    total = placed[5]
    for k in (4, 3, 2, 1):
        hi, lo = halves(total)
        got = widen(k, jnp.concatenate([hi, lo], axis=0))
        col = lax.broadcasted_iota(jnp.int32, (1, PAD[k]), 1) - (HALO >> k) + me * (N >> k)
        ok = (col >= 0) & (col < n_lvl * (N >> k))
        total = placed[k] + jnp.where(ok, got[0:192] + got[192:384], 0.0)
        if k in (4, 3):
            band(3, 5 - k)
    hi, lo = halves(total)
    got = dot(pick, hi[:, 128:512])
    lows = []
    for j, there in ((2, q2), (1, q1), (3, q3)):
        low[j - 1] = got[64 * j : 64 * j + 64].astype(BF)
        lows.append(remote(low.at[j - 1], there, n_send.at[j - 1], n_recv.at[j - 1], others[j]))
    lowo[...] = got[0:64] + dot(pick[0:64], lo[:, 128:512])
    copies = [pltpu.make_async_copy(lowo, own_out, out_sem.at[0])]
    copies[0].start()
    for i, t in ((0, 0), (1, 3)):
        cols = slice(128 * t, 128 * t + 256)
        wide = dot(jnp.concatenate([hi[:, cols], lo[:, cols]], axis=0), e0[...])
        b_hi, b_lo = halves(wide[0:192] + wide[192:384])
        for ch in range(3):
            r = slice(64 * ch, 64 * ch + 64)
            got = dot(last, jnp.concatenate([kept[i, ch], b_hi[r], b_lo[r]], axis=0))
            lateo[i, ch] = got[0:32]
            for j in (1, 2, 3):
                late[i, j - 1, ch] = got[32 * j : 32 * j + 32].astype(BF)
        for j, there in ((2, l2), (1, l1), (3, l3)):
            lows.append(remote(late.at[i, j - 1], there.at[i], p_send.at[i, j - 1], p_recv.at[i, j - 1], others[j]))
    copies.append(pltpu.make_async_copy(lateo, late_out, out_sem.at[2]))
    copies[1].start()

    for copy in sends:
        copy.wait_recv()
    for t in range(2):
        base[:, :, 256 * t : 256 * t + 256] = (sent[t, 0] + got_in[t, 1]) + (got_in[t, 2] + got_in[t, 3])
    copies.append(pltpu.make_async_copy(base, base_out, out_sem.at[1]))
    copies[2].start()
    for copy in sends:
        copy.wait_send()
    for copy in lows:
        copy.wait()
    for copy in copies:
        copy.wait()


def finish(base, low, late, q1, q2, q3, l1, l2, l3, e0, tall, out):
    for i, t in ((0, 0), (1, 3)):
        out[:, :, 256 * t : 256 * t + 256] = late[i] + (l2[i].astype(F32) + (l1[i].astype(F32) + l3[i].astype(F32)))
    total = low[...] + (q2[...].astype(F32) + (q1[...].astype(F32) + q3[...].astype(F32)))
    hi, lo = halves(total)
    hi, lo = halves(dot(tall[...], jnp.concatenate([hi, lo], axis=0)))
    for t in (0, 1):
        cols = slice(128 * t, 128 * t + 256)
        got = dot(jnp.concatenate([hi[:, cols], lo[:, cols]], axis=0), e0[...])
        cols = slice(256 * t, 256 * t + 256)
        out[:, :, 256 + 256 * t : 512 + 256 * t] = base[:, :, cols].astype(F32) + (got[0:96] + got[96:192]).reshape(3, 32, 256)


def solution(mesh):
    n_strip, n_lvl = mesh.shape["strip"], mesh.shape["lvl"]
    table = constants()

    def per_device(photos, seams, offsets):
        far = pl.BlockSpec(memory_space=pltpu.HBM)
        given = [jnp.asarray(table[name]) for name in NAMES]
        dma = pltpu.SemaphoreType.DMA
        tile = (4, 3, 32, 256)
        strip = (3, 32, N)
        low_shape = jax.ShapeDtypeStruct((64, 384), BF)
        late_shape = jax.ShapeDtypeStruct((2, 3, 32, 256), BF)
        results = pl.pallas_call(
            functools.partial(kernel, n_strip, n_lvl),
            out_shape=(
                jax.ShapeDtypeStruct((3, 32, 512), BF),
                jax.ShapeDtypeStruct((64, 384), F32),
                jax.ShapeDtypeStruct((2, 3, 32, 256), F32),
                *[low_shape] * 3,
                *[late_shape] * 3,
            ),
            in_specs=[far] * (3 + len(NAMES)),
            out_specs=(far,) * 9,
            scratch_shapes=[
                *[pltpu.VMEM(a.shape[1:] if name == "h35" else a.shape, a.dtype) for name, a in zip(NAMES, given)],
                dma((len(NAMES) + 5,)),
                pltpu.VMEM((4, 3, 64, N), BF),
                pltpu.SMEM((4,), jnp.int32),
                pltpu.VMEM((4, 2, 64), jnp.int32),
                pltpu.VMEM((256, 128), F32),
                pltpu.VMEM((256, 128), F32),
                pltpu.VMEM((4, 128, 1280), BF),
                pltpu.VMEM((512, 640), BF),
                pltpu.VMEM((512, 640), BF),
                pltpu.VMEM((512, 384), BF),
                pltpu.VMEM((256, 1280), BF),
                pltpu.VMEM((4, 384, 256), BF),
                pltpu.VMEM((4, 384, 256), BF),
                pltpu.VMEM((2, *tile), BF),
                pltpu.VMEM((2, *tile), BF),
                pltpu.VMEM((3, 32, 512), BF),
                pltpu.VMEM((3, 64, 384), BF),
                pltpu.VMEM((64, 384), F32),
                pltpu.VMEM((2, 3, 256, 256), BF),
                pltpu.VMEM((2, 3, 3, 32, 256), BF),
                pltpu.VMEM((2, 3, 32, 256), F32),
                dma((3,)),
                *[dma((2,))] * 2,
                dma((2, 3)), dma((2, 3)), dma((3,)), dma((3,)), dma((2, 3)), dma((2, 3)),
            ],
            compiler_params=pltpu.CompilerParams(collective_id=0, has_side_effects=True),
        )(offsets, photos, seams, *given)
        near = pl.BlockSpec(memory_space=pltpu.VMEM)
        return pl.pallas_call(
            finish, out_shape=jax.ShapeDtypeStruct(strip, F32), in_specs=[near] * 11, out_specs=near
        )(*results, jnp.asarray(table["e0"]), jnp.asarray(table["tall"]))

    placed = (P("strip", None, None, "lvl"), P("strip", None, None), P("strip"))
    return jax.shard_map(
        per_device, mesh=mesh, in_specs=placed, out_specs=P(None, "strip", "lvl"), check_vma=False
    )
```

```python
import functools

import jax
import jax.numpy as jnp
import ml_dtypes
import numpy as np
from jax import lax
from jax.experimental import pallas as pl
from jax.experimental.pallas import tpu as pltpu
from jax.sharding import PartitionSpec as P

BF = jnp.bfloat16
F32 = jnp.float32
MESH = pl.DeviceIdType.MESH
TAPS = (0.0625, 0.25, 0.375, 0.25, 0.0625)
N = 1024
HALO = 128
WIDE = {0: 1280, 1: 640, 2: 320, 3: 160, 4: 80, 5: 40}
PAD = {1: 640, 2: 384, 3: 256, 4: 128, 5: 128}
ROWS = {0: 64, 1: 32, 2: 16, 3: 8, 4: 4, 5: 2}
SLOT = {2: (0, 64), 3: (64, 32), 4: (96, 16), 5: (112, 16)}


def reduce_rows(tall):
    m = np.zeros((tall // 2, tall))
    for i in range(tall // 2):
        for t in range(5):
            r = 2 * i + t - 2
            if 0 <= r < tall:
                m[i, r] = TAPS[t]
    return m


def expand_rows(tall):
    m = np.zeros((2 * tall, tall))
    for i in range(tall):
        for r, w in ((i - 1, 0.125), (i, 0.75), (i + 1, 0.125)):
            if 0 <= r < tall:
                m[2 * i, r] = w
        for r in (i, i + 1):
            if r < tall:
                m[2 * i + 1, r] = 0.5
    return m


def blocks(m, count):
    return np.kron(np.eye(count), m)


def bf(x):
    return np.asarray(x, np.float32).astype(ml_dtypes.bfloat16)


def split(x):
    hi = bf(x)
    return hi, bf(np.asarray(x, np.float64) - hi.astype(np.float64))


def valid(level, edge):
    e = np.arange(WIDE[level])
    h = HALO >> level
    n = N >> level
    keep = np.ones(WIDE[level])
    if edge == 0:
        keep[e < h] = 0
    if edge == 2:
        keep[e >= h + n] = 0
    return keep


def reduce_cols(level, edge):
    m = reduce_rows(WIDE[level]).T
    return m * valid(level + 1, edge)[None, :]


def constants():
    c = {}
    c["v1"] = bf(blocks(reduce_rows(64), 4))
    w = np.zeros((512, 128))
    for col in range(128):
        for t in range(5):
            w[128 + 2 * col + t - 2, col] = TAPS[t]
    c["wred"] = bf(w)
    v = {1: np.eye(32)}
    for k in (2, 3, 4, 5):
        v[k] = reduce_rows(ROWS[k - 1]) @ v[k - 1]
    v25 = np.zeros((128, 128))
    for k in (2, 3, 4, 5):
        start, _ = SLOT[k]
        v25[start : start + 4 * ROWS[k]] = blocks(v[k], 4)
    c["v25"] = bf(v25)
    h35 = np.zeros((3, 384, 384))
    for edge in range(3):
        m3 = reduce_cols(2, edge)
        m4 = m3 @ reduce_cols(3, edge)
        m5 = m4 @ reduce_cols(4, edge)
        h35[edge, :320, 0:160] = m3
        h35[edge, :320, 256:336] = m4
        h35[edge, :320, 336:376] = m5
    c["h35"] = bf(h35)
    c["er1"] = bf(blocks(expand_rows(16), 12))
    c["er2"] = bf(blocks(expand_rows(8), 12))
    c["er3"] = bf(blocks(expand_rows(4), 12))
    er4 = np.zeros((48, 48))
    for ch in range(3):
        er4[16 * ch : 16 * ch + 16, 16 * ch : 16 * ch + 8] = blocks(expand_rows(2), 4)
    c["er4"] = bf(er4)
    for k in (1, 2, 3, 4):
        m = np.zeros((PAD[k + 1], PAD[k]))
        at = 80 if k == 4 else 0
        m[at : at + WIDE[k + 1], : WIDE[k]] = expand_rows(WIDE[k + 1]).T
        if k == 1:
            c["ec1a"], c["ec1b"] = bf(m[0:256, 0:384]), bf(m[128:384, 384:640])
        else:
            c[f"ec{k}"] = bf(m)
    e0 = np.zeros((256, 256))
    for col in range(256):
        i = 64 + col // 2
        if col % 2 == 0:
            e0[i - 1, col], e0[i, col], e0[i + 1, col] = 0.125, 0.75, 0.125
        else:
            e0[i, col], e0[i + 1, col] = 0.5, 0.5
    c["e0"] = bf(e0)
    er0 = blocks(expand_rows(32), 4)
    one = expand_rows(18)[2:34]
    tall = np.zeros((96, 64))
    for ch in range(3):
        tall[32 * ch : 32 * ch + 32, 18 * ch : 18 * ch + 18] = one
    c["tall"] = bf(np.concatenate([tall, tall], axis=1))
    c["d0"] = bf(np.concatenate([er0, er0], axis=1))
    hi = np.zeros((3, 64, 640))
    lo = np.zeros((3, 64, 640))
    for first in range(3):
        up = np.eye(64)
        for k in (1, 2, 3, 4, 5):
            h = 32 >> k
            if k > 1:
                up = up @ expand_rows(4 * h)
            place = np.zeros((4 * h, 2 * h))
            place[first * h : first * h + 2 * h] = np.eye(2 * h)
            m = np.tile(up @ place, (1, 4))
            a, b = split(m)
            s = 128 * (k - 1)
            hi[first, :, s : s + m.shape[1]] = a.astype(np.float64)
            lo[first, :, s : s + m.shape[1]] = b.astype(np.float64)
    c["lb"] = bf(hi)
    c["lb5"] = bf(lo[:, :, 384:])
    assert not lo[:, :, :384].any()
    pm = np.full((8, 640), -1.0)
    for k in (1, 2, 3, 4, 5):
        for p in range(4):
            s = 128 * (k - 1) + p * ROWS[k]
            pm[:, s : s + ROWS[k]] = p
    c["pm"] = pm.astype(np.float32)
    return c


NAMES = ("v1", "wred", "v25", "h35", "er1", "er2", "er3", "er4", "ec1a", "ec1b", "ec2", "ec3", "ec4", "e0", "d0", "lb", "lb5", "pm")


def dot(a, b):
    return jnp.dot(a, b, preferred_element_type=F32)


def halves(x):
    hi = x.astype(BF)
    return hi, (x - hi.astype(F32)).astype(BF)


def kernel(n_strip, n_lvl, offsets_in, photos_in, seams_in, *refs):
    n = len(NAMES)
    given, outs, held, rest = refs[:n], refs[n : n + 9], refs[n + 9 : 2 * n + 9], refs[2 * n + 9 :]
    body(n_strip, n_lvl, offsets_in, photos_in, seams_in, dict(zip(NAMES, given)), *outs, dict(zip(NAMES, held)), *rest)


def body(n_strip, n_lvl, offsets_in, photos_in, seams_in, given, base_out, own_out, late_out, q1, q2, q3, l1, l2, l3, held, load, photos, offsets, seams, s0, s1, tm, g1,
         ys, y2, mk, uh, ul, sent, got_in, base, low, lowo, kept, late, lateo, out_sem,
         halo_send, halo_recv, m_send, m_recv, n_send, n_recv, p_send, p_recv):
    x = lax.axis_index("strip")
    me = lax.axis_index("lvl")
    right, left = lax.rem(me + 1, n_lvl), lax.rem(me + n_lvl - 1, n_lvl)
    others = [lax.rem(x + j, n_strip) for j in range(n_strip)]
    barrier = pltpu.get_barrier_semaphore()
    for target in ({"lvl": left}, {"lvl": right}, {"strip": others[1]}, {"strip": others[2]}, {"strip": others[3]}):
        pl.semaphore_signal(barrier, inc=1, device_id=target, device_id_type=MESH)
    edge = jnp.where(me == 0, 0, jnp.where(me == n_lvl - 1, 2, 1))
    waits = {}

    def fetch(name, src, dst):
        copy = pltpu.make_async_copy(src, dst, load.at[len(waits)])
        copy.start()
        waits[name] = copy

    def ready(name):
        if waits[name] is not None:
            waits[name].wait()
            waits[name] = None

    def const(name):
        ready(name)
        return held[name]

    fetch("seams", seams_in, seams)
    fetch("v1", given["v1"], held["v1"])
    for name, at, width in (("west", 0, 128), ("east", N - 128, 128), ("middle", 128, N - 256)):
        cols = slice(at, at + width)
        fetch(name, photos_in.at[:, :, :, cols], photos.at[:, :, :, cols])
    fetch("offsets", offsets_in, offsets)
    for name in NAMES[1:]:
        fetch(name, given[name].at[edge] if name == "h35" else given[name], held[name])

    def rows_of(ch, start, width):
        return photos[:, ch, :, start : start + width].reshape(256, width)

    lead = const("v1")[...]
    ready("west")
    ready("east")
    for start in (0, N - 128):
        for ch in range(3):
            tm[ch, :, HALO + start : HALO + start + 128] = dot(lead, rows_of(ch, start, 128)).astype(BF)
    r_i = lax.broadcasted_iota(jnp.int32, (64, 64), 0)
    c_i = lax.broadcasted_iota(jnp.int32, (64, 64), 1)
    eye = r_i == c_i
    ready("seams")
    for p in range(4):
        for e, dst in ((0, s0), (1, s1)):
            line = seams[p, e : e + 1, :].astype(F32)
            col = jnp.sum(jnp.where(eye, line, 0.0), axis=1, keepdims=True)
            dst[64 * p : 64 * p + 64, :] = jnp.broadcast_to(col, (64, 128))

    first_col = (me * N).astype(F32)

    def mask_tile(start):
        col = lax.broadcasted_iota(jnp.int32, (256, 128), 1).astype(F32) + (first_col + (start - HALO))
        a, b = s0[...], s1[...]
        return jnp.concatenate([(c >= a) & (c < b) for c in (col, col + 128.0)], axis=1)

    for start in range(0, N + 256, 256):
        m = jnp.where(mask_tile(start), 1.0, 0.0).astype(BF)
        mk[:, start : start + 256] = m
        tm[3, :, start : start + 256] = dot(lead, m).astype(BF)
    pl.semaphore_wait(barrier, 5)
    halo = []
    for i, (src, dst, target) in enumerate(((HALO, HALO + N, left), (N, 0, right))):
        copy = pltpu.make_async_remote_copy(
            src_ref=tm.at[0:3, :, src : src + 128],
            dst_ref=tm.at[0:3, :, dst : dst + 128],
            send_sem=halo_send.at[i],
            recv_sem=halo_recv.at[i],
            device_id={"lvl": target},
            device_id_type=MESH,
        )
        copy.start()
        halo.append(copy)
    ready("middle")
    for ch in range(3):
        tm[ch, :, 256 : N] = dot(lead, rows_of(ch, 128, N - 256)).astype(BF)

    wred = const("wred")

    def g1_tile(j, lo=0, hi=4):
        a, b = max(0, 2 * j - 1), min(10, 2 * j + 3)
        w = wred[128 * (a - 2 * j + 1) : 128 * (b - 2 * j + 1), :]
        val = dot(tm[lo:hi, :, 128 * a : 128 * b].reshape(128 * (hi - lo), 128 * (b - a)), w)
        if j in (0, 4):
            col = lax.broadcasted_iota(jnp.int32, (1, 128), 1) + (128 * j - 64) + me * (N // 2)
            val = jnp.where((col >= 0) & (col < n_lvl * (N // 2)), val, 0.0)
        g1[128 * lo : 128 * hi, 128 * j : 128 * j + 128] = val.astype(BF)

    for j in (1, 2):
        g1_tile(j)
    e0, d0 = const("e0"), const("d0")
    ready("offsets")
    places = [offsets[p] for p in range(4)]

    q = lax.broadcasted_iota(jnp.int32, (128, 256), 0)
    lane = lax.broadcasted_iota(jnp.int32, (128, 256), 1)
    where = jnp.where(lane < 64, places[0], jnp.where(lane < 128, places[1], jnp.where(lane < 192, places[2], places[3])))
    put = jnp.where((((q >> 5) + x) & 3) * 32 + (q & 31) == where * 32 + (lane & 63), 1.0, 0.0).astype(BF)

    def remote(src, dst, send, recv, target):
        copy = pltpu.make_async_remote_copy(
            src_ref=src, dst_ref=dst, send_sem=send, recv_sem=recv, device_id={"strip": target}, device_id_type=MESH
        )
        copy.start()
        return copy

    sends = []

    def widened(t):
        hi, lo = halves(dot(g1[0:384, 128 * t : 128 * t + 256], e0[...]))
        uh[t], ul[t] = hi, lo

    def band(t, ch):
        r = slice(128 * ch, 128 * ch + 128)
        away = dot(d0[...], jnp.concatenate([uh[t, r], ul[t, r]], axis=0))
        detail = rows_of(ch, 256 * t, 256).astype(F32) - away
        weighted_0 = detail.astype(BF) * mk[:, HALO + 256 * t : HALO + 256 * t + 256]
        kept[t, ch] = weighted_0

    def place(t, ch):
        got = dot(put, kept[t, ch]).astype(BF)
        for j in range(4):
            sent[t - 1, j, ch] = got[32 * j : 32 * j + 32]

    def send_band(t):
        for j in (2, 1, 3):
            k = j - 1
            sends.append(remote(sent.at[t - 1, j], got_in.at[t - 1, j], m_send.at[t - 1, k], m_recv.at[t - 1, k], others[j]))

    col2 = lax.broadcasted_iota(jnp.int32, (1, 384), 1) - 32 + me * (N // 4)
    inside2 = (col2 >= 0) & (col2 < n_lvl * (N // 4))

    def deep(lo, hi):
        count = hi - lo
        rows = slice(128 * lo, 128 * hi)
        for ch in range(lo, hi):
            ys[128 * ch : 128 * ch + 128, :] = dot(held["v25"][...], g1[128 * ch : 128 * ch + 128, :]).astype(BF)
        yield
        for j, a, b in ((0, 0, 3), (1, 1, 5), (2, 3, 5)):
            w = wred[128 * (a - 2 * j + 1) : 128 * (b - 2 * j + 1), :]
            val = dot(ys[rows, 128 * a : 128 * b], w)
            y2[rows, 128 * j : 128 * j + 128] = jnp.where(inside2[:, 128 * j : 128 * j + 128], val, 0.0).astype(BF)
        yield
        y = y2[rows, :].reshape(count, 128, 384)
        y35 = dot(y[:, 64:128].reshape(64 * count, 384), held["h35"][...]).astype(BF).reshape(count, 64, 384)
        yield {
            1: g1[rows, :],
            2: y[:, 0:64].reshape(64 * count, 384),
            3: y35[:, 0:32, 0:256].reshape(32 * count, 256),
            4: y35[:, 32:48, 256:384].reshape(16 * count, 128),
            5: y35[:, 48:64, 256:384].reshape(16 * count, 128),
        }

    g1_tile(3)
    widened(1)
    widened(2)
    band(1, 0)
    band(1, 1)
    place(1, 0)
    band(1, 2)
    place(1, 1)
    place(1, 2)
    send_band(1)
    band(2, 0)
    band(2, 1)
    place(2, 0)
    band(2, 2)
    place(2, 1)
    place(2, 2)
    send_band(2)
    for name in NAMES:
        ready(name)
    pm, lb, lb5 = held["pm"], held["lb"], held["lb5"]

    def by_photo(which):
        got = jnp.zeros(which.shape, F32)
        for p in range(4):
            got = jnp.where(which == float(p), places[p].astype(F32), got)
        return got

    spot = by_photo(pm[0:1, :])
    table = sum(jnp.where(spot == float(o), lb[o].astype(F32), 0.0) for o in range(3)).astype(BF)
    fine = sum(jnp.where(spot[:, 384:] == float(o), lb5[o].astype(F32), 0.0) for o in range(3)).astype(BF)
    q = lax.broadcasted_iota(jnp.int32, (128, 128), 0)
    row = (((q >> 5) + x) & 3) * 32 + (q & 31)
    d = (lax.broadcasted_iota(jnp.int32, (128, 128), 1) & 63) - (row >> 1)
    even = jnp.where(d == 0, 0.75, jnp.where((d == 1) | (d == -1), 0.125, 0.0))
    odd = jnp.where((d == 0) | (d == 1), 0.5, 0.0)
    last = jnp.concatenate([put, jnp.where((row & 1) == 0, even, odd).astype(BF)], axis=1)

    q = lax.broadcasted_iota(jnp.int32, (256, 192), 0)
    k = lax.broadcasted_iota(jnp.int32, (256, 192), 1)
    rest = q & 63
    chan = jnp.where(rest >= 18, 1, 0) + jnp.where(rest >= 36, 1, 0)
    row = (((q >> 6) + x) & 3) * 16 + rest - 18 * chan - 1
    pick = jnp.where((rest < 54) & (row == (k & 63)) & (chan == (k >> 6)), 1.0, 0.0).astype(BF)
    for copy in halo:
        copy.wait()
    for at, outer in ((0, 0), (N + 128, n_lvl - 1)):
        tm[0:3, :, at : at + 128] = jnp.where(me == outer, jnp.zeros((), BF), tm[0:3, :, at : at + 128])
    for t in (0, 3):
        g1_tile(0 if t == 0 else 4)
        widened(t)

    colors, masks = deep(0, 3), deep(3, 4)
    next(colors)
    next(masks)
    band(0, 0)
    next(colors)
    next(masks)
    band(0, 1)
    gs = next(colors)
    ms = next(masks)

    weighted = {}
    er = {k: const(f"er{k}") for k in (1, 2, 3, 4)}

    def widen(k, field):
        if k == 1:
            return jnp.concatenate([dot(field[:, 0:256], held["ec1a"][...]), dot(field[:, 128:384], held["ec1b"][...])], axis=1)
        return dot(field, held[f"ec{k}"][...])

    for k, color in ((4, 48), (3, 48), (2, 96), (1, 192)):
        tall = 4 * ROWS[k]
        rough = dot(er[k][...], gs[k + 1][0:color])
        expanded = widen(k, jnp.concatenate(halves(rough), axis=0))
        expanded = expanded[: 3 * tall] + expanded[3 * tall :]
        m = ms[k].astype(F32)
        detail = gs[k].astype(F32) - expanded
        weighted[k] = [(m * detail[ch * tall : ch * tall + tall]).astype(BF) for ch in range(3)]
    weighted[5] = [(ms[5].astype(F32) * gs[5][16 * ch : 16 * ch + 16].astype(F32)).astype(BF) for ch in range(3)]

    band(0, 2)
    band(3, 0)
    placed = {}
    for k in (5, 4, 3, 2, 1):
        s = 128 * (k - 1)
        size = {1: 128, 2: 64, 3: 32, 4: 16, 5: 16}[k]
        lhs = table[:, s : s + size]
        if k >= 4:
            lhs = jnp.concatenate([lhs, fine[:, s - 384 : s - 384 + size]], axis=0)
        parts = []
        for ch in range(3):
            got = dot(lhs, weighted[k][ch])
            parts.append(got[0:64] + got[64:128] if k >= 4 else got)
        placed[k] = jnp.concatenate(parts, axis=0)

    total = placed[5]
    for k in (4, 3, 2, 1):
        hi, lo = halves(total)
        got = widen(k, jnp.concatenate([hi, lo], axis=0))
        col = lax.broadcasted_iota(jnp.int32, (1, PAD[k]), 1) - (HALO >> k) + me * (N >> k)
        ok = (col >= 0) & (col < n_lvl * (N >> k))
        total = placed[k] + jnp.where(ok, got[0:192] + got[192:384], 0.0)
        if k in (4, 3):
            band(3, 5 - k)
    hi, lo = halves(total)
    got = dot(pick, hi[:, 128:512])
    lows = []
    for j, there in ((2, q2), (1, q1), (3, q3)):
        low[j - 1] = got[64 * j : 64 * j + 64].astype(BF)
        lows.append(remote(low.at[j - 1], there, n_send.at[j - 1], n_recv.at[j - 1], others[j]))
    lowo[...] = got[0:64] + dot(pick[0:64], lo[:, 128:512])
    copies = [pltpu.make_async_copy(lowo, own_out, out_sem.at[0])]
    copies[0].start()
    grown = []
    for t in (0, 3):
        cols = slice(128 * t, 128 * t + 256)
        wide = dot(jnp.concatenate([hi[:, cols], lo[:, cols]], axis=0), e0[...])
        grown.append(halves(wide[0:192] + wide[192:384]))
    for i, t in ((0, 0), (1, 3)):
        b_hi, b_lo = grown[i]
        for ch in range(3):
            r = slice(64 * ch, 64 * ch + 64)
            got = dot(last, jnp.concatenate([kept[t, ch], b_hi[r], b_lo[r]], axis=0))
            lateo[i, ch] = got[0:32]
            for j in (1, 2, 3):
                late[i, j - 1, ch] = got[32 * j : 32 * j + 32].astype(BF)
        for j, there in ((2, l2), (1, l1), (3, l3)):
            lows.append(remote(late.at[i, j - 1], there.at[i], p_send.at[i, j - 1], p_recv.at[i, j - 1], others[j]))
    copies.append(pltpu.make_async_copy(lateo, late_out, out_sem.at[2]))
    copies[1].start()

    for copy in sends:
        copy.wait_recv()
    for t in range(2):
        base[:, :, 256 * t : 256 * t + 256] = (sent[t, 0] + got_in[t, 1]) + (got_in[t, 2] + got_in[t, 3])
    copies.append(pltpu.make_async_copy(base, base_out, out_sem.at[1]))
    copies[2].start()
    for copy in sends:
        copy.wait_send()
    for copy in lows:
        copy.wait()
    for copy in copies:
        copy.wait()


def finish(base, low, late, q1, q2, q3, l1, l2, l3, e0, tall, out):
    for i, t in ((0, 0), (1, 3)):
        out[:, :, 256 * t : 256 * t + 256] = late[i] + (l2[i].astype(F32) + (l1[i].astype(F32) + l3[i].astype(F32)))
    total = low[...] + (q2[...].astype(F32) + (q1[...].astype(F32) + q3[...].astype(F32)))
    hi, lo = halves(total)
    hi, lo = halves(dot(tall[...], jnp.concatenate([hi, lo], axis=0)))
    for t in (0, 1):
        cols = slice(128 * t, 128 * t + 256)
        got = dot(jnp.concatenate([hi[:, cols], lo[:, cols]], axis=0), e0[...])
        cols = slice(256 * t, 256 * t + 256)
        out[:, :, 256 + 256 * t : 512 + 256 * t] = base[:, :, cols].astype(F32) + (got[0:96] + got[96:192]).reshape(3, 32, 256)


def solution(mesh):
    n_strip, n_lvl = mesh.shape["strip"], mesh.shape["lvl"]
    table = constants()

    def per_device(photos, seams, offsets):
        far = pl.BlockSpec(memory_space=pltpu.HBM)
        given = [jnp.asarray(table[name]) for name in NAMES]
        dma = pltpu.SemaphoreType.DMA
        tile = (4, 3, 32, 256)
        strip = (3, 32, N)
        low_shape = jax.ShapeDtypeStruct((64, 384), BF)
        late_shape = jax.ShapeDtypeStruct((2, 3, 32, 256), BF)
        results = pl.pallas_call(
            functools.partial(kernel, n_strip, n_lvl),
            out_shape=(
                jax.ShapeDtypeStruct((3, 32, 512), BF),
                jax.ShapeDtypeStruct((64, 384), F32),
                jax.ShapeDtypeStruct((2, 3, 32, 256), F32),
                *[low_shape] * 3,
                *[late_shape] * 3,
            ),
            in_specs=[far] * (3 + len(NAMES)),
            out_specs=(far,) * 9,
            scratch_shapes=[
                *[pltpu.VMEM(a.shape[1:] if name == "h35" else a.shape, a.dtype) for name, a in zip(NAMES, given)],
                dma((len(NAMES) + 5,)),
                pltpu.VMEM((4, 3, 64, N), BF),
                pltpu.SMEM((4,), jnp.int32),
                pltpu.VMEM((4, 2, 64), jnp.int32),
                pltpu.VMEM((256, 128), F32),
                pltpu.VMEM((256, 128), F32),
                pltpu.VMEM((4, 128, 1280), BF),
                pltpu.VMEM((512, 640), BF),
                pltpu.VMEM((512, 640), BF),
                pltpu.VMEM((512, 384), BF),
                pltpu.VMEM((256, 1280), BF),
                pltpu.VMEM((4, 384, 256), BF),
                pltpu.VMEM((4, 384, 256), BF),
                pltpu.VMEM((2, *tile), BF),
                pltpu.VMEM((2, *tile), BF),
                pltpu.VMEM((3, 32, 512), BF),
                pltpu.VMEM((3, 64, 384), BF),
                pltpu.VMEM((64, 384), F32),
                pltpu.VMEM((4, 3, 256, 256), BF),
                pltpu.VMEM((2, 3, 3, 32, 256), BF),
                pltpu.VMEM((2, 3, 32, 256), F32),
                dma((3,)),
                *[dma((2,))] * 2,
                dma((2, 3)), dma((2, 3)), dma((3,)), dma((3,)), dma((2, 3)), dma((2, 3)),
            ],
            compiler_params=pltpu.CompilerParams(collective_id=0, has_side_effects=True),
        )(offsets, photos, seams, *given)
        near = pl.BlockSpec(memory_space=pltpu.VMEM)
        return pl.pallas_call(
            finish, out_shape=jax.ShapeDtypeStruct(strip, F32), in_specs=[near] * 11, out_specs=near
        )(*results, jnp.asarray(table["e0"]), jnp.asarray(table["tall"]))

    placed = (P("strip", None, None, "lvl"), P("strip", None, None), P("strip"))
    return jax.shard_map(
        per_device, mesh=mesh, in_specs=placed, out_specs=P(None, "strip", "lvl"), check_vma=False
    )
```

```python
import functools

import jax
import jax.numpy as jnp
import ml_dtypes
import numpy as np
from jax import lax
from jax.experimental import pallas as pl
from jax.experimental.pallas import tpu as pltpu
from jax.sharding import PartitionSpec as P

BF = jnp.bfloat16
F32 = jnp.float32
MESH = pl.DeviceIdType.MESH
TAPS = (0.0625, 0.25, 0.375, 0.25, 0.0625)
N = 1024
HALO = 128
WIDE = {0: 1280, 1: 640, 2: 320, 3: 160, 4: 80, 5: 40}
PAD = {1: 640, 2: 384, 3: 256, 4: 128, 5: 128}
ROWS = {0: 64, 1: 32, 2: 16, 3: 8, 4: 4, 5: 2}
SLOT = {2: (0, 64), 3: (64, 32), 4: (96, 16), 5: (112, 16)}


def reduce_rows(tall):
    m = np.zeros((tall // 2, tall))
    for i in range(tall // 2):
        for t in range(5):
            r = 2 * i + t - 2
            if 0 <= r < tall:
                m[i, r] = TAPS[t]
    return m


def expand_rows(tall):
    m = np.zeros((2 * tall, tall))
    for i in range(tall):
        for r, w in ((i - 1, 0.125), (i, 0.75), (i + 1, 0.125)):
            if 0 <= r < tall:
                m[2 * i, r] = w
        for r in (i, i + 1):
            if r < tall:
                m[2 * i + 1, r] = 0.5
    return m


def blocks(m, count):
    return np.kron(np.eye(count), m)


def bf(x):
    return np.asarray(x, np.float32).astype(ml_dtypes.bfloat16)


def split(x):
    hi = bf(x)
    return hi, bf(np.asarray(x, np.float64) - hi.astype(np.float64))


def valid(level, edge):
    e = np.arange(WIDE[level])
    h = HALO >> level
    n = N >> level
    keep = np.ones(WIDE[level])
    if edge == 0:
        keep[e < h] = 0
    if edge == 2:
        keep[e >= h + n] = 0
    return keep


def reduce_cols(level, edge):
    m = reduce_rows(WIDE[level]).T
    return m * valid(level + 1, edge)[None, :]


def constants():
    c = {}
    c["v1"] = bf(blocks(reduce_rows(64), 4))
    w = np.zeros((512, 128))
    for col in range(128):
        for t in range(5):
            w[128 + 2 * col + t - 2, col] = TAPS[t]
    c["wred"] = bf(w)
    v = {1: np.eye(32)}
    for k in (2, 3, 4, 5):
        v[k] = reduce_rows(ROWS[k - 1]) @ v[k - 1]
    v25 = np.zeros((128, 128))
    for k in (2, 3, 4, 5):
        start, _ = SLOT[k]
        v25[start : start + 4 * ROWS[k]] = blocks(v[k], 4)
    c["v25"] = bf(v25)
    h35 = np.zeros((3, 384, 384))
    for edge in range(3):
        m3 = reduce_cols(2, edge)
        m4 = m3 @ reduce_cols(3, edge)
        m5 = m4 @ reduce_cols(4, edge)
        h35[edge, :320, 0:160] = m3
        h35[edge, :320, 256:336] = m4
        h35[edge, :320, 336:376] = m5
    c["h35"] = bf(h35)
    c["er1"] = bf(blocks(expand_rows(16), 12))
    c["er2"] = bf(blocks(expand_rows(8), 12))
    c["er3"] = bf(blocks(expand_rows(4), 12))
    er4 = np.zeros((48, 48))
    for ch in range(3):
        er4[16 * ch : 16 * ch + 16, 16 * ch : 16 * ch + 8] = blocks(expand_rows(2), 4)
    c["er4"] = bf(er4)
    for k in (1, 2, 3, 4):
        m = np.zeros((PAD[k + 1], PAD[k]))
        at = 80 if k == 4 else 0
        m[at : at + WIDE[k + 1], : WIDE[k]] = expand_rows(WIDE[k + 1]).T
        if k == 1:
            c["ec1a"], c["ec1b"] = bf(m[0:256, 0:384]), bf(m[128:384, 384:640])
        else:
            c[f"ec{k}"] = bf(m)
    e0 = np.zeros((256, 256))
    for col in range(256):
        i = 64 + col // 2
        if col % 2 == 0:
            e0[i - 1, col], e0[i, col], e0[i + 1, col] = 0.125, 0.75, 0.125
        else:
            e0[i, col], e0[i + 1, col] = 0.5, 0.5
    c["e0"] = bf(e0)
    er0 = blocks(expand_rows(32), 4)
    one = expand_rows(18)[2:34]
    tall = np.zeros((96, 64))
    for ch in range(3):
        tall[32 * ch : 32 * ch + 32, 18 * ch : 18 * ch + 18] = one
    c["tall"] = bf(np.concatenate([tall, tall], axis=1))
    c["d0"] = bf(np.concatenate([er0, er0], axis=1))
    hi = np.zeros((3, 64, 640))
    lo = np.zeros((3, 64, 640))
    for first in range(3):
        up = np.eye(64)
        for k in (1, 2, 3, 4, 5):
            h = 32 >> k
            if k > 1:
                up = up @ expand_rows(4 * h)
            place = np.zeros((4 * h, 2 * h))
            place[first * h : first * h + 2 * h] = np.eye(2 * h)
            m = np.tile(up @ place, (1, 4))
            a, b = split(m)
            s = 128 * (k - 1)
            hi[first, :, s : s + m.shape[1]] = a.astype(np.float64)
            lo[first, :, s : s + m.shape[1]] = b.astype(np.float64)
    c["lb"] = bf(hi)
    c["lb5"] = bf(lo[:, :, 384:])
    assert not lo[:, :, :384].any()
    pm = np.full((8, 640), -1.0)
    for k in (1, 2, 3, 4, 5):
        for p in range(4):
            s = 128 * (k - 1) + p * ROWS[k]
            pm[:, s : s + ROWS[k]] = p
    c["pm"] = pm.astype(np.float32)
    return c


NAMES = ("v1", "wred", "v25", "h35", "er1", "er2", "er3", "er4", "ec1a", "ec1b", "ec2", "ec3", "ec4", "e0", "d0", "lb", "lb5", "pm")


def dot(a, b):
    return jnp.dot(a, b, preferred_element_type=F32)


def halves(x):
    hi = x.astype(BF)
    return hi, (x - hi.astype(F32)).astype(BF)


def kernel(n_strip, n_lvl, offsets_in, photos_in, seams_in, *refs):
    n = len(NAMES)
    given, outs, held, rest = refs[:n], refs[n : n + 9], refs[n + 9 : 2 * n + 9], refs[2 * n + 9 :]
    body(n_strip, n_lvl, offsets_in, photos_in, seams_in, dict(zip(NAMES, given)), *outs, dict(zip(NAMES, held)), *rest)


def body(n_strip, n_lvl, offsets_in, photos_in, seams_in, given, base_out, own_out, late_out, q1, q2, q3, l1, l2, l3, held, load, photos, offsets, seams, s0, s1, tm, g1,
         ys, y2, mk, uh, ul, sent, got_in, base, low, lowo, kept, late, lateo, out_sem,
         halo_send, halo_recv, m_send, m_recv, n_send, n_recv, p_send, p_recv):
    x = lax.axis_index("strip")
    me = lax.axis_index("lvl")
    right, left = lax.rem(me + 1, n_lvl), lax.rem(me + n_lvl - 1, n_lvl)
    others = [lax.rem(x + j, n_strip) for j in range(n_strip)]
    barrier = pltpu.get_barrier_semaphore()
    for target in ({"lvl": left}, {"lvl": right}, {"strip": others[1]}, {"strip": others[2]}, {"strip": others[3]}):
        pl.semaphore_signal(barrier, inc=1, device_id=target, device_id_type=MESH)
    edge = jnp.where(me == 0, 0, jnp.where(me == n_lvl - 1, 2, 1))
    waits = {}

    def fetch(name, src, dst):
        copy = pltpu.make_async_copy(src, dst, load.at[len(waits)])
        copy.start()
        waits[name] = copy

    def ready(name):
        if waits[name] is not None:
            waits[name].wait()
            waits[name] = None

    def const(name):
        ready(name)
        return held[name]

    fetch("seams", seams_in, seams)
    fetch("v1", given["v1"], held["v1"])
    for name, at, width in (("west", 0, 128), ("east", N - 128, 128), ("middle", 128, N - 256)):
        cols = slice(at, at + width)
        fetch(name, photos_in.at[:, :, :, cols], photos.at[:, :, :, cols])
    fetch("offsets", offsets_in, offsets)
    for name in NAMES[1:]:
        fetch(name, given[name].at[edge] if name == "h35" else given[name], held[name])

    def rows_of(ch, start, width):
        return photos[:, ch, :, start : start + width].reshape(256, width)

    lead = const("v1")[...]
    ready("west")
    ready("east")
    for start in (0, N - 128):
        for ch in range(3):
            tm[ch, :, HALO + start : HALO + start + 128] = dot(lead, rows_of(ch, start, 128)).astype(BF)
    r_i = lax.broadcasted_iota(jnp.int32, (64, 64), 0)
    c_i = lax.broadcasted_iota(jnp.int32, (64, 64), 1)
    eye = r_i == c_i
    ready("seams")
    for p in range(4):
        for e, dst in ((0, s0), (1, s1)):
            line = seams[p, e : e + 1, :].astype(F32)
            col = jnp.sum(jnp.where(eye, line, 0.0), axis=1, keepdims=True)
            dst[64 * p : 64 * p + 64, :] = jnp.broadcast_to(col, (64, 128))

    first_col = (me * N).astype(F32)

    def mask_tile(start):
        col = lax.broadcasted_iota(jnp.int32, (256, 128), 1).astype(F32) + (first_col + (start - HALO))
        a, b = s0[...], s1[...]
        return jnp.concatenate([(c >= a) & (c < b) for c in (col, col + 128.0)], axis=1)

    for start in range(0, N + 256, 256):
        m = jnp.where(mask_tile(start), 1.0, 0.0).astype(BF)
        mk[:, start : start + 256] = m
        tm[3, :, start : start + 256] = dot(lead, m).astype(BF)
    pl.semaphore_wait(barrier, 5)
    halo = []
    for i, (src, dst, target) in enumerate(((HALO, HALO + N, left), (N, 0, right))):
        copy = pltpu.make_async_remote_copy(
            src_ref=tm.at[0:3, :, src : src + 128],
            dst_ref=tm.at[0:3, :, dst : dst + 128],
            send_sem=halo_send.at[i],
            recv_sem=halo_recv.at[i],
            device_id={"lvl": target},
            device_id_type=MESH,
        )
        copy.start()
        halo.append(copy)
    ready("middle")
    for ch in range(3):
        tm[ch, :, 256 : N] = dot(lead, rows_of(ch, 128, N - 256)).astype(BF)

    wred = const("wred")

    def g1_tile(j, lo=0, hi=4):
        a, b = max(0, 2 * j - 1), min(10, 2 * j + 3)
        w = wred[128 * (a - 2 * j + 1) : 128 * (b - 2 * j + 1), :]
        val = dot(tm[lo:hi, :, 128 * a : 128 * b].reshape(128 * (hi - lo), 128 * (b - a)), w)
        if j in (0, 4):
            col = lax.broadcasted_iota(jnp.int32, (1, 128), 1) + (128 * j - 64) + me * (N // 2)
            val = jnp.where((col >= 0) & (col < n_lvl * (N // 2)), val, 0.0)
        g1[128 * lo : 128 * hi, 128 * j : 128 * j + 128] = val.astype(BF)

    for j in (1, 2):
        g1_tile(j)
    e0, d0 = const("e0"), const("d0")
    ready("offsets")
    places = [offsets[p] for p in range(4)]

    q = lax.broadcasted_iota(jnp.int32, (128, 256), 0)
    lane = lax.broadcasted_iota(jnp.int32, (128, 256), 1)
    where = jnp.where(lane < 64, places[0], jnp.where(lane < 128, places[1], jnp.where(lane < 192, places[2], places[3])))
    put = jnp.where((((q >> 5) + x) & 3) * 32 + (q & 31) == where * 32 + (lane & 63), 1.0, 0.0).astype(BF)

    def remote(src, dst, send, recv, target):
        copy = pltpu.make_async_remote_copy(
            src_ref=src, dst_ref=dst, send_sem=send, recv_sem=recv, device_id={"strip": target}, device_id_type=MESH
        )
        copy.start()
        return copy

    sends = []

    def widened(t):
        hi, lo = halves(dot(g1[0:384, 128 * t : 128 * t + 256], e0[...]))
        uh[t], ul[t] = hi, lo

    def band(t, ch):
        r = slice(128 * ch, 128 * ch + 128)
        away = dot(d0[...], jnp.concatenate([uh[t, r], ul[t, r]], axis=0))
        detail = rows_of(ch, 256 * t, 256).astype(F32) - away
        weighted_0 = detail.astype(BF) * mk[:, HALO + 256 * t : HALO + 256 * t + 256]
        kept[t, ch] = weighted_0

    def place(t, ch):
        got = dot(put, kept[t, ch]).astype(BF)
        for j in range(4):
            sent[t - 1, j, ch] = got[32 * j : 32 * j + 32]

    def send_band(t):
        for j in (2, 1, 3):
            k = j - 1
            sends.append(remote(sent.at[t - 1, j], got_in.at[t - 1, j], m_send.at[t - 1, k], m_recv.at[t - 1, k], others[j]))

    col2 = lax.broadcasted_iota(jnp.int32, (1, 384), 1) - 32 + me * (N // 4)
    inside2 = (col2 >= 0) & (col2 < n_lvl * (N // 4))

    def deep(lo, hi):
        count = hi - lo
        rows = slice(128 * lo, 128 * hi)
        for ch in range(lo, hi):
            ys[128 * ch : 128 * ch + 128, :] = dot(held["v25"][...], g1[128 * ch : 128 * ch + 128, :]).astype(BF)
        yield
        for j, a, b in ((0, 0, 3), (1, 1, 5), (2, 3, 5)):
            w = wred[128 * (a - 2 * j + 1) : 128 * (b - 2 * j + 1), :]
            val = dot(ys[rows, 128 * a : 128 * b], w)
            y2[rows, 128 * j : 128 * j + 128] = jnp.where(inside2[:, 128 * j : 128 * j + 128], val, 0.0).astype(BF)
        yield
        y = y2[rows, :].reshape(count, 128, 384)
        y35 = dot(y[:, 64:128].reshape(64 * count, 384), held["h35"][...]).astype(BF).reshape(count, 64, 384)
        yield {
            1: g1[rows, :],
            2: y[:, 0:64].reshape(64 * count, 384),
            3: y35[:, 0:32, 0:256].reshape(32 * count, 256),
            4: y35[:, 32:48, 256:384].reshape(16 * count, 128),
            5: y35[:, 48:64, 256:384].reshape(16 * count, 128),
        }

    g1_tile(3)
    widened(1)
    widened(2)
    band(1, 0)
    band(1, 1)
    place(1, 0)
    band(1, 2)
    place(1, 1)
    place(1, 2)
    send_band(1)
    band(2, 0)
    band(2, 1)
    place(2, 0)
    band(2, 2)
    place(2, 1)
    place(2, 2)
    send_band(2)
    for name in NAMES:
        ready(name)
    pm, lb, lb5 = held["pm"], held["lb"], held["lb5"]

    def by_photo(which):
        got = jnp.zeros(which.shape, F32)
        for p in range(4):
            got = jnp.where(which == float(p), places[p].astype(F32), got)
        return got

    spot = by_photo(pm[0:1, :])
    table = sum(jnp.where(spot == float(o), lb[o].astype(F32), 0.0) for o in range(3)).astype(BF)
    fine = sum(jnp.where(spot[:, 384:] == float(o), lb5[o].astype(F32), 0.0) for o in range(3)).astype(BF)
    q = lax.broadcasted_iota(jnp.int32, (128, 128), 0)
    row = (((q >> 5) + x) & 3) * 32 + (q & 31)
    d = (lax.broadcasted_iota(jnp.int32, (128, 128), 1) & 63) - (row >> 1)
    even = jnp.where(d == 0, 0.75, jnp.where((d == 1) | (d == -1), 0.125, 0.0))
    odd = jnp.where((d == 0) | (d == 1), 0.5, 0.0)
    last = jnp.concatenate([put, jnp.where((row & 1) == 0, even, odd).astype(BF)], axis=1)

    q = lax.broadcasted_iota(jnp.int32, (256, 192), 0)
    k = lax.broadcasted_iota(jnp.int32, (256, 192), 1)
    rest = q & 63
    chan = jnp.where(rest >= 18, 1, 0) + jnp.where(rest >= 36, 1, 0)
    row = (((q >> 6) + x) & 3) * 16 + rest - 18 * chan - 1
    pick = jnp.where((rest < 54) & (row == (k & 63)) & (chan == (k >> 6)), 1.0, 0.0).astype(BF)
    for copy in halo:
        copy.wait()
    for at, outer in ((0, 0), (N + 128, n_lvl - 1)):
        tm[0:3, :, at : at + 128] = jnp.where(me == outer, jnp.zeros((), BF), tm[0:3, :, at : at + 128])
    for t in (0, 3):
        g1_tile(0 if t == 0 else 4)
        widened(t)

    colors, masks = deep(0, 3), deep(3, 4)
    next(colors)
    next(masks)
    band(0, 0)
    next(colors)
    next(masks)
    band(0, 1)
    gs = next(colors)
    ms = next(masks)

    weighted = {}
    er = {k: const(f"er{k}") for k in (1, 2, 3, 4)}

    def widen(k, field):
        if k == 1:
            return jnp.concatenate([dot(field[:, 0:256], held["ec1a"][...]), dot(field[:, 128:384], held["ec1b"][...])], axis=1)
        return dot(field, held[f"ec{k}"][...])

    for k, color in ((4, 48), (3, 48), (2, 96), (1, 192)):
        tall = 4 * ROWS[k]
        rough = dot(er[k][...], gs[k + 1][0:color])
        expanded = widen(k, jnp.concatenate(halves(rough), axis=0))
        expanded = expanded[: 3 * tall] + expanded[3 * tall :]
        m = ms[k].astype(F32)
        detail = gs[k].astype(F32) - expanded
        weighted[k] = [(m * detail[ch * tall : ch * tall + tall]).astype(BF) for ch in range(3)]
    weighted[5] = [(ms[5].astype(F32) * gs[5][16 * ch : 16 * ch + 16].astype(F32)).astype(BF) for ch in range(3)]

    band(0, 2)
    band(3, 0)
    placed = {}
    for k in (5, 4, 3, 2, 1):
        s = 128 * (k - 1)
        size = {1: 128, 2: 64, 3: 32, 4: 16, 5: 16}[k]
        lhs = table[:, s : s + size]
        if k >= 4:
            lhs = jnp.concatenate([lhs, fine[:, s - 384 : s - 384 + size]], axis=0)
        parts = []
        for ch in range(3):
            got = dot(lhs, weighted[k][ch])
            parts.append(got[0:64] + got[64:128] if k >= 4 else got)
        placed[k] = jnp.concatenate(parts, axis=0)

    total = placed[5]
    for k in (4, 3, 2, 1):
        hi, lo = halves(total)
        got = widen(k, jnp.concatenate([hi, lo], axis=0))
        col = lax.broadcasted_iota(jnp.int32, (1, PAD[k]), 1) - (HALO >> k) + me * (N >> k)
        ok = (col >= 0) & (col < n_lvl * (N >> k))
        total = placed[k] + jnp.where(ok, got[0:192] + got[192:384], 0.0)
        if k in (4, 3):
            band(3, 5 - k)
    hi, lo = halves(total)
    got = dot(pick, hi[:, 128:512])
    lows = []
    for j, there in ((2, q2), (1, q1), (3, q3)):
        low[j - 1] = got[64 * j : 64 * j + 64].astype(BF)
        lows.append(remote(low.at[j - 1], there, n_send.at[j - 1], n_recv.at[j - 1], others[j]))
    lowo[...] = got[0:64] + dot(pick[0:64], lo[:, 128:512])
    copies = [pltpu.make_async_copy(lowo, own_out, out_sem.at[0])]
    copies[0].start()
    for i, t in ((0, 0), (1, 3)):
        cols = slice(128 * t, 128 * t + 256)
        wide = dot(jnp.concatenate([hi[:, cols], lo[:, cols]], axis=0), e0[...])
        b_hi, b_lo = halves(wide[0:192] + wide[192:384])
        for ch in range(3):
            r = slice(64 * ch, 64 * ch + 64)
            got = dot(last, jnp.concatenate([kept[t, ch], b_hi[r], b_lo[r]], axis=0))
            lateo[i, ch] = got[0:32]
            for j in (1, 2, 3):
                late[i, j - 1, ch] = got[32 * j : 32 * j + 32].astype(BF)
        for j, there in ((2, l2), (1, l1), (3, l3)):
            lows.append(remote(late.at[i, j - 1], there.at[i], p_send.at[i, j - 1], p_recv.at[i, j - 1], others[j]))
    copies.append(pltpu.make_async_copy(lateo, late_out, out_sem.at[2]))
    copies[1].start()

    for copy in sends:
        copy.wait_recv()
    for t in range(2):
        base[:, :, 256 * t : 256 * t + 256] = (sent[t, 0] + got_in[t, 1]) + (got_in[t, 2] + got_in[t, 3])
    copies.append(pltpu.make_async_copy(base, base_out, out_sem.at[1]))
    copies[2].start()
    for copy in sends:
        copy.wait_send()
    for copy in lows:
        copy.wait()
    for copy in copies:
        copy.wait()


def finish(base, low, late, q1, q2, q3, l1, l2, l3, e0, tall, out):
    for i, t in ((0, 0), (1, 3)):
        out[:, :, 256 * t : 256 * t + 256] = late[i] + (l2[i].astype(F32) + (l1[i].astype(F32) + l3[i].astype(F32)))
    total = low[...] + (q2[...].astype(F32) + (q1[...].astype(F32) + q3[...].astype(F32)))
    hi, lo = halves(total)
    hi, lo = halves(dot(tall[...], jnp.concatenate([hi, lo], axis=0)))
    for t in (0, 1):
        cols = slice(128 * t, 128 * t + 256)
        got = dot(jnp.concatenate([hi[:, cols], lo[:, cols]], axis=0), e0[...])
        cols = slice(256 * t, 256 * t + 256)
        out[:, :, 256 + 256 * t : 512 + 256 * t] = base[:, :, cols].astype(F32) + (got[0:96] + got[96:192]).reshape(3, 32, 256)


def solution(mesh):
    n_strip, n_lvl = mesh.shape["strip"], mesh.shape["lvl"]
    table = constants()

    def per_device(photos, seams, offsets):
        far = pl.BlockSpec(memory_space=pltpu.HBM)
        given = [jnp.asarray(table[name]) for name in NAMES]
        dma = pltpu.SemaphoreType.DMA
        tile = (4, 3, 32, 256)
        strip = (3, 32, N)
        low_shape = jax.ShapeDtypeStruct((64, 384), BF)
        late_shape = jax.ShapeDtypeStruct((2, 3, 32, 256), BF)
        results = pl.pallas_call(
            functools.partial(kernel, n_strip, n_lvl),
            out_shape=(
                jax.ShapeDtypeStruct((3, 32, 512), BF),
                jax.ShapeDtypeStruct((64, 384), F32),
                jax.ShapeDtypeStruct((2, 3, 32, 256), F32),
                *[low_shape] * 3,
                *[late_shape] * 3,
            ),
            in_specs=[far] * (3 + len(NAMES)),
            out_specs=(far,) * 9,
            scratch_shapes=[
                *[pltpu.VMEM(a.shape[1:] if name == "h35" else a.shape, a.dtype) for name, a in zip(NAMES, given)],
                dma((len(NAMES) + 5,)),
                pltpu.VMEM((4, 3, 64, N), BF),
                pltpu.SMEM((4,), jnp.int32),
                pltpu.VMEM((4, 2, 64), jnp.int32),
                pltpu.VMEM((256, 128), F32),
                pltpu.VMEM((256, 128), F32),
                pltpu.VMEM((4, 128, 1280), BF),
                pltpu.VMEM((512, 640), BF),
                pltpu.VMEM((512, 640), BF),
                pltpu.VMEM((512, 384), BF),
                pltpu.VMEM((256, 1280), BF),
                pltpu.VMEM((4, 384, 256), BF),
                pltpu.VMEM((4, 384, 256), BF),
                pltpu.VMEM((2, *tile), BF),
                pltpu.VMEM((2, *tile), BF),
                pltpu.VMEM((3, 32, 512), BF),
                pltpu.VMEM((3, 64, 384), BF),
                pltpu.VMEM((64, 384), F32),
                pltpu.VMEM((4, 3, 256, 256), BF),
                pltpu.VMEM((2, 3, 3, 32, 256), BF),
                pltpu.VMEM((2, 3, 32, 256), F32),
                dma((3,)),
                *[dma((2,))] * 2,
                dma((2, 3)), dma((2, 3)), dma((3,)), dma((3,)), dma((2, 3)), dma((2, 3)),
            ],
            compiler_params=pltpu.CompilerParams(collective_id=0, has_side_effects=True),
        )(offsets, photos, seams, *given)
        near = pl.BlockSpec(memory_space=pltpu.VMEM)
        return pl.pallas_call(
            finish, out_shape=jax.ShapeDtypeStruct(strip, F32), in_specs=[near] * 11, out_specs=near
        )(*results, jnp.asarray(table["e0"]), jnp.asarray(table["tall"]))

    placed = (P("strip", None, None, "lvl"), P("strip", None, None), P("strip"))
    return jax.shard_map(
        per_device, mesh=mesh, in_specs=placed, out_specs=P(None, "strip", "lvl"), check_vma=False
    )
```

```python
import functools

import jax
import jax.numpy as jnp
import ml_dtypes
import numpy as np
from jax import lax
from jax.experimental import pallas as pl
from jax.experimental.pallas import tpu as pltpu
from jax.sharding import PartitionSpec as P

BF = jnp.bfloat16
F32 = jnp.float32
MESH = pl.DeviceIdType.MESH
TAPS = (0.0625, 0.25, 0.375, 0.25, 0.0625)
N = 1024
HALO = 128
WIDE = {0: 1280, 1: 640, 2: 320, 3: 160, 4: 80, 5: 40}
PAD = {1: 640, 2: 384, 3: 256, 4: 128, 5: 128}
ROWS = {0: 64, 1: 32, 2: 16, 3: 8, 4: 4, 5: 2}
SLOT = {2: (0, 64), 3: (64, 32), 4: (96, 16), 5: (112, 16)}


def reduce_rows(tall):
    m = np.zeros((tall // 2, tall))
    for i in range(tall // 2):
        for t in range(5):
            r = 2 * i + t - 2
            if 0 <= r < tall:
                m[i, r] = TAPS[t]
    return m


def expand_rows(tall):
    m = np.zeros((2 * tall, tall))
    for i in range(tall):
        for r, w in ((i - 1, 0.125), (i, 0.75), (i + 1, 0.125)):
            if 0 <= r < tall:
                m[2 * i, r] = w
        for r in (i, i + 1):
            if r < tall:
                m[2 * i + 1, r] = 0.5
    return m


def blocks(m, count):
    return np.kron(np.eye(count), m)


def bf(x):
    return np.asarray(x, np.float32).astype(ml_dtypes.bfloat16)


def split(x):
    hi = bf(x)
    return hi, bf(np.asarray(x, np.float64) - hi.astype(np.float64))


def valid(level, edge):
    e = np.arange(WIDE[level])
    h = HALO >> level
    n = N >> level
    keep = np.ones(WIDE[level])
    if edge == 0:
        keep[e < h] = 0
    if edge == 2:
        keep[e >= h + n] = 0
    return keep


def reduce_cols(level, edge):
    m = reduce_rows(WIDE[level]).T
    return m * valid(level + 1, edge)[None, :]


def constants():
    c = {}
    c["v1"] = bf(blocks(reduce_rows(64), 4))
    w = np.zeros((512, 128))
    for col in range(128):
        for t in range(5):
            w[128 + 2 * col + t - 2, col] = TAPS[t]
    c["wred"] = bf(w)
    v = {1: np.eye(32)}
    for k in (2, 3, 4, 5):
        v[k] = reduce_rows(ROWS[k - 1]) @ v[k - 1]
    v25 = np.zeros((128, 128))
    for k in (2, 3, 4, 5):
        start, _ = SLOT[k]
        v25[start : start + 4 * ROWS[k]] = blocks(v[k], 4)
    c["v25"] = bf(v25)
    h35 = np.zeros((3, 384, 384))
    for edge in range(3):
        m3 = reduce_cols(2, edge)
        m4 = m3 @ reduce_cols(3, edge)
        m5 = m4 @ reduce_cols(4, edge)
        h35[edge, :320, 0:160] = m3
        h35[edge, :320, 256:336] = m4
        h35[edge, :320, 336:376] = m5
    c["h35"] = bf(h35)
    c["er1"] = bf(blocks(expand_rows(16), 12))
    c["er2"] = bf(blocks(expand_rows(8), 12))
    c["er3"] = bf(blocks(expand_rows(4), 12))
    er4 = np.zeros((48, 48))
    for ch in range(3):
        er4[16 * ch : 16 * ch + 16, 16 * ch : 16 * ch + 8] = blocks(expand_rows(2), 4)
    c["er4"] = bf(er4)
    for k in (1, 2, 3, 4):
        m = np.zeros((PAD[k + 1], PAD[k]))
        at = 80 if k == 4 else 0
        m[at : at + WIDE[k + 1], : WIDE[k]] = expand_rows(WIDE[k + 1]).T
        if k == 1:
            c["ec1a"], c["ec1b"] = bf(m[0:256, 0:384]), bf(m[128:384, 384:640])
        else:
            c[f"ec{k}"] = bf(m)
    e0 = np.zeros((256, 256))
    for col in range(256):
        i = 64 + col // 2
        if col % 2 == 0:
            e0[i - 1, col], e0[i, col], e0[i + 1, col] = 0.125, 0.75, 0.125
        else:
            e0[i, col], e0[i + 1, col] = 0.5, 0.5
    c["e0"] = bf(e0)
    er0 = blocks(expand_rows(32), 4)
    one = expand_rows(18)[2:34]
    tall = np.zeros((96, 64))
    for ch in range(3):
        tall[32 * ch : 32 * ch + 32, 18 * ch : 18 * ch + 18] = one
    c["tall"] = bf(np.concatenate([tall, tall], axis=1))
    c["d0"] = bf(np.concatenate([er0, er0], axis=1))
    hi = np.zeros((3, 64, 640))
    lo = np.zeros((3, 64, 640))
    for first in range(3):
        up = np.eye(64)
        for k in (1, 2, 3, 4, 5):
            h = 32 >> k
            if k > 1:
                up = up @ expand_rows(4 * h)
            place = np.zeros((4 * h, 2 * h))
            place[first * h : first * h + 2 * h] = np.eye(2 * h)
            m = np.tile(up @ place, (1, 4))
            a, b = split(m)
            s = 128 * (k - 1)
            hi[first, :, s : s + m.shape[1]] = a.astype(np.float64)
            lo[first, :, s : s + m.shape[1]] = b.astype(np.float64)
    c["lb"] = bf(hi)
    c["lb5"] = bf(lo[:, :, 384:])
    assert not lo[:, :, :384].any()
    pm = np.full((8, 640), -1.0)
    for k in (1, 2, 3, 4, 5):
        for p in range(4):
            s = 128 * (k - 1) + p * ROWS[k]
            pm[:, s : s + ROWS[k]] = p
    c["pm"] = pm.astype(np.float32)
    return c


NAMES = ("v1", "wred", "v25", "h35", "er1", "er2", "er3", "er4", "ec1a", "ec1b", "ec2", "ec3", "ec4", "e0", "d0", "lb", "lb5", "pm")


def dot(a, b):
    return jnp.dot(a, b, preferred_element_type=F32)


def halves(x):
    hi = x.astype(BF)
    return hi, (x - hi.astype(F32)).astype(BF)


def kernel(n_strip, n_lvl, offsets_in, photos_in, seams_in, *refs):
    n = len(NAMES)
    given, outs, held, rest = refs[:n], refs[n : n + 9], refs[n + 9 : 2 * n + 9], refs[2 * n + 9 :]
    body(n_strip, n_lvl, offsets_in, photos_in, seams_in, dict(zip(NAMES, given)), *outs, dict(zip(NAMES, held)), *rest)


def body(n_strip, n_lvl, offsets_in, photos_in, seams_in, given, base_out, own_out, late_out, q1, q2, q3, l1, l2, l3, held, load, photos, offsets, seams, s0, s1, tm, g1,
         ys, y2, mk, uh, ul, sent, got_in, base, low, lowo, kept, late, lateo, out_sem,
         halo_send, halo_recv, m_send, m_recv, n_send, n_recv, p_send, p_recv):
    x = lax.axis_index("strip")
    me = lax.axis_index("lvl")
    right, left = lax.rem(me + 1, n_lvl), lax.rem(me + n_lvl - 1, n_lvl)
    others = [lax.rem(x + j, n_strip) for j in range(n_strip)]
    barrier = pltpu.get_barrier_semaphore()
    for target in ({"lvl": left}, {"lvl": right}, {"strip": others[1]}, {"strip": others[2]}, {"strip": others[3]}):
        pl.semaphore_signal(barrier, inc=1, device_id=target, device_id_type=MESH)
    edge = jnp.where(me == 0, 0, jnp.where(me == n_lvl - 1, 2, 1))
    waits = {}

    def fetch(name, src, dst):
        copy = pltpu.make_async_copy(src, dst, load.at[len(waits)])
        copy.start()
        waits[name] = copy

    def ready(name):
        if waits[name] is not None:
            waits[name].wait()
            waits[name] = None

    def const(name):
        ready(name)
        return held[name]

    fetch("seams", seams_in, seams)
    fetch("v1", given["v1"], held["v1"])
    for name, at, width in (("west", 0, 128), ("east", N - 128, 128), ("middle", 128, N - 256)):
        cols = slice(at, at + width)
        fetch(name, photos_in.at[:, :, :, cols], photos.at[:, :, :, cols])
    fetch("offsets", offsets_in, offsets)
    for name in NAMES[1:]:
        fetch(name, given[name].at[edge] if name == "h35" else given[name], held[name])

    def rows_of(ch, start, width):
        return photos[:, ch, :, start : start + width].reshape(256, width)

    lead = const("v1")[...]
    ready("west")
    ready("east")
    for start in (0, N - 128):
        for ch in range(3):
            tm[ch, :, HALO + start : HALO + start + 128] = dot(lead, rows_of(ch, start, 128)).astype(BF)
    r_i = lax.broadcasted_iota(jnp.int32, (64, 64), 0)
    c_i = lax.broadcasted_iota(jnp.int32, (64, 64), 1)
    eye = r_i == c_i
    ready("seams")
    for p in range(4):
        for e, dst in ((0, s0), (1, s1)):
            line = seams[p, e : e + 1, :].astype(F32)
            col = jnp.sum(jnp.where(eye, line, 0.0), axis=1, keepdims=True)
            dst[64 * p : 64 * p + 64, :] = jnp.broadcast_to(col, (64, 128))

    first_col = (me * N).astype(F32)

    def mask_tile(start):
        col = lax.broadcasted_iota(jnp.int32, (256, 128), 1).astype(F32) + (first_col + (start - HALO))
        a, b = s0[...], s1[...]
        return jnp.concatenate([(c >= a) & (c < b) for c in (col, col + 128.0)], axis=1)

    for start in range(0, N + 256, 256):
        m = jnp.where(mask_tile(start), 1.0, 0.0).astype(BF)
        mk[:, start : start + 256] = m
        tm[3, :, start : start + 256] = dot(lead, m).astype(BF)
    pl.semaphore_wait(barrier, 5)
    halo = []
    for i, (src, dst, target) in enumerate(((HALO, HALO + N, left), (N, 0, right))):
        copy = pltpu.make_async_remote_copy(
            src_ref=tm.at[0:3, :, src : src + 128],
            dst_ref=tm.at[0:3, :, dst : dst + 128],
            send_sem=halo_send.at[i],
            recv_sem=halo_recv.at[i],
            device_id={"lvl": target},
            device_id_type=MESH,
        )
        copy.start()
        halo.append(copy)
    ready("middle")
    for ch in range(3):
        tm[ch, :, 256 : N] = dot(lead, rows_of(ch, 128, N - 256)).astype(BF)

    wred = const("wred")

    def g1_tile(j, lo=0, hi=4):
        a, b = max(0, 2 * j - 1), min(10, 2 * j + 3)
        w = wred[128 * (a - 2 * j + 1) : 128 * (b - 2 * j + 1), :]
        val = dot(tm[lo:hi, :, 128 * a : 128 * b].reshape(128 * (hi - lo), 128 * (b - a)), w)
        if j in (0, 4):
            col = lax.broadcasted_iota(jnp.int32, (1, 128), 1) + (128 * j - 64) + me * (N // 2)
            val = jnp.where((col >= 0) & (col < n_lvl * (N // 2)), val, 0.0)
        g1[128 * lo : 128 * hi, 128 * j : 128 * j + 128] = val.astype(BF)

    for j in (1, 2):
        g1_tile(j)
    e0, d0 = const("e0"), const("d0")
    ready("offsets")
    places = [offsets[p] for p in range(4)]

    q = lax.broadcasted_iota(jnp.int32, (128, 256), 0)
    lane = lax.broadcasted_iota(jnp.int32, (128, 256), 1)
    where = jnp.where(lane < 64, places[0], jnp.where(lane < 128, places[1], jnp.where(lane < 192, places[2], places[3])))
    put = jnp.where((((q >> 5) + x) & 3) * 32 + (q & 31) == where * 32 + (lane & 63), 1.0, 0.0).astype(BF)

    def remote(src, dst, send, recv, target):
        copy = pltpu.make_async_remote_copy(
            src_ref=src, dst_ref=dst, send_sem=send, recv_sem=recv, device_id={"strip": target}, device_id_type=MESH
        )
        copy.start()
        return copy

    sends = []

    def widened(t):
        hi, lo = halves(dot(g1[0:384, 128 * t : 128 * t + 256], e0[...]))
        uh[t], ul[t] = hi, lo

    def band(t, ch):
        r = slice(128 * ch, 128 * ch + 128)
        away = dot(d0[...], jnp.concatenate([uh[t, r], ul[t, r]], axis=0))
        detail = rows_of(ch, 256 * t, 256).astype(F32) - away
        weighted_0 = detail.astype(BF) * mk[:, HALO + 256 * t : HALO + 256 * t + 256]
        kept[t, ch] = weighted_0

    def place(t, ch):
        got = dot(put, kept[t, ch]).astype(BF)
        for j in range(4):
            sent[t - 1, j, ch] = got[32 * j : 32 * j + 32]

    def send_band(t):
        for j in (2, 1, 3):
            k = j - 1
            sends.append(remote(sent.at[t - 1, j], got_in.at[t - 1, j], m_send.at[t - 1, k], m_recv.at[t - 1, k], others[j]))

    col2 = lax.broadcasted_iota(jnp.int32, (1, 384), 1) - 32 + me * (N // 4)
    inside2 = (col2 >= 0) & (col2 < n_lvl * (N // 4))

    def deep(lo, hi):
        count = hi - lo
        rows = slice(128 * lo, 128 * hi)
        for ch in range(lo, hi):
            ys[128 * ch : 128 * ch + 128, :] = dot(held["v25"][...], g1[128 * ch : 128 * ch + 128, :]).astype(BF)
        yield
        for j, a, b in ((0, 0, 3), (1, 1, 5), (2, 3, 5)):
            w = wred[128 * (a - 2 * j + 1) : 128 * (b - 2 * j + 1), :]
            val = dot(ys[rows, 128 * a : 128 * b], w)
            y2[rows, 128 * j : 128 * j + 128] = jnp.where(inside2[:, 128 * j : 128 * j + 128], val, 0.0).astype(BF)
        yield
        y = y2[rows, :].reshape(count, 128, 384)
        y35 = dot(y[:, 64:128].reshape(64 * count, 384), held["h35"][...]).astype(BF).reshape(count, 64, 384)
        yield {
            1: g1[rows, :],
            2: y[:, 0:64].reshape(64 * count, 384),
            3: y35[:, 0:32, 0:256].reshape(32 * count, 256),
            4: y35[:, 32:48, 256:384].reshape(16 * count, 128),
            5: y35[:, 48:64, 256:384].reshape(16 * count, 128),
        }

    g1_tile(3)
    widened(1)
    widened(2)
    band(1, 0)
    band(1, 1)
    place(1, 0)
    band(1, 2)
    place(1, 1)
    place(1, 2)
    send_band(1)
    band(2, 0)
    band(2, 1)
    place(2, 0)
    band(2, 2)
    place(2, 1)
    place(2, 2)
    send_band(2)
    for name in NAMES:
        ready(name)
    pm, lb, lb5 = held["pm"], held["lb"], held["lb5"]

    def by_photo(which):
        got = jnp.zeros(which.shape, F32)
        for p in range(4):
            got = jnp.where(which == float(p), places[p].astype(F32), got)
        return got

    spot = by_photo(pm[0:1, :])
    table = sum(jnp.where(spot == float(o), lb[o].astype(F32), 0.0) for o in range(3)).astype(BF)
    fine = sum(jnp.where(spot[:, 384:] == float(o), lb5[o].astype(F32), 0.0) for o in range(3)).astype(BF)
    q = lax.broadcasted_iota(jnp.int32, (128, 128), 0)
    row = (((q >> 5) + x) & 3) * 32 + (q & 31)
    d = (lax.broadcasted_iota(jnp.int32, (128, 128), 1) & 63) - (row >> 1)
    even = jnp.where(d == 0, 0.75, jnp.where((d == 1) | (d == -1), 0.125, 0.0))
    odd = jnp.where((d == 0) | (d == 1), 0.5, 0.0)
    last = jnp.concatenate([put, jnp.where((row & 1) == 0, even, odd).astype(BF)], axis=1)

    q = lax.broadcasted_iota(jnp.int32, (256, 192), 0)
    k = lax.broadcasted_iota(jnp.int32, (256, 192), 1)
    rest = q & 63
    chan = jnp.where(rest >= 18, 1, 0) + jnp.where(rest >= 36, 1, 0)
    row = (((q >> 6) + x) & 3) * 16 + rest - 18 * chan - 1
    pick = jnp.where((rest < 54) & (row == (k & 63)) & (chan == (k >> 6)), 1.0, 0.0).astype(BF)
    for copy in halo:
        copy.wait()
    for at, outer in ((0, 0), (N + 128, n_lvl - 1)):
        tm[0:3, :, at : at + 128] = jnp.where(me == outer, jnp.zeros((), BF), tm[0:3, :, at : at + 128])
    for t in (0, 3):
        g1_tile(0 if t == 0 else 4)
        widened(t)

    colors, masks = deep(0, 3), deep(3, 4)
    next(colors)
    next(masks)
    band(0, 0)
    next(colors)
    next(masks)
    band(0, 1)
    gs = next(colors)
    ms = next(masks)

    weighted = {}
    er = {k: const(f"er{k}") for k in (1, 2, 3, 4)}

    def widen(k, field):
        if k == 1:
            return jnp.concatenate([dot(field[:, 0:256], held["ec1a"][...]), dot(field[:, 128:384], held["ec1b"][...])], axis=1)
        return dot(field, held[f"ec{k}"][...])

    for k, color in ((4, 48), (3, 48), (2, 96), (1, 192)):
        tall = 4 * ROWS[k]
        rough = dot(er[k][...], gs[k + 1][0:color])
        expanded = widen(k, jnp.concatenate(halves(rough), axis=0))
        expanded = expanded[: 3 * tall] + expanded[3 * tall :]
        m = ms[k].astype(F32)
        detail = gs[k].astype(F32) - expanded
        weighted[k] = [(m * detail[ch * tall : ch * tall + tall]).astype(BF) for ch in range(3)]
    weighted[5] = [(ms[5].astype(F32) * gs[5][16 * ch : 16 * ch + 16].astype(F32)).astype(BF) for ch in range(3)]

    band(0, 2)
    band(3, 0)
    placed = {}
    for k in (5, 4, 3, 2, 1):
        s = 128 * (k - 1)
        size = {1: 128, 2: 64, 3: 32, 4: 16, 5: 16}[k]
        lhs = table[:, s : s + size]
        if k >= 4:
            lhs = jnp.concatenate([lhs, fine[:, s - 384 : s - 384 + size]], axis=0)
        parts = []
        for ch in range(3):
            got = dot(lhs, weighted[k][ch])
            parts.append(got[0:64] + got[64:128] if k >= 4 else got)
        placed[k] = jnp.concatenate(parts, axis=0)

    total = placed[5]
    for k in (4, 3, 2, 1):
        hi, lo = halves(total)
        got = widen(k, jnp.concatenate([hi, lo], axis=0))
        col = lax.broadcasted_iota(jnp.int32, (1, PAD[k]), 1) - (HALO >> k) + me * (N >> k)
        ok = (col >= 0) & (col < n_lvl * (N >> k))
        total = placed[k] + jnp.where(ok, got[0:192] + got[192:384], 0.0)
        if k in (4, 3):
            band(3, 5 - k)
    hi, lo = halves(total)
    got = dot(pick, hi[:, 128:512])
    lows = []
    for j, there in ((2, q2), (1, q1), (3, q3)):
        low[j - 1] = got[64 * j : 64 * j + 64].astype(BF)
        lows.append(remote(low.at[j - 1], there, n_send.at[j - 1], n_recv.at[j - 1], others[j]))
    lowo[...] = got[0:64]
    for i, t in ((0, 0), (1, 3)):
        cols = slice(128 * t, 128 * t + 256)
        wide = dot(jnp.concatenate([hi[:, cols], lo[:, cols]], axis=0), e0[...])
        b_hi, b_lo = halves(wide[0:192] + wide[192:384])
        for ch in range(3):
            r = slice(64 * ch, 64 * ch + 64)
            got = dot(last, jnp.concatenate([kept[t, ch], b_hi[r], b_lo[r]], axis=0))
            lateo[i, ch] = got[0:32]
            for j in (1, 2, 3):
                late[i, j - 1, ch] = got[32 * j : 32 * j + 32].astype(BF)
        for j, there in ((2, l2), (1, l1), (3, l3)):
            lows.append(remote(late.at[i, j - 1], there.at[i], p_send.at[i, j - 1], p_recv.at[i, j - 1], others[j]))
    lowo[...] = lowo[...] + dot(pick[0:64], lo[:, 128:512])
    copies = [pltpu.make_async_copy(lowo, own_out, out_sem.at[0])]
    copies[0].start()
    copies.append(pltpu.make_async_copy(lateo, late_out, out_sem.at[2]))
    copies[1].start()

    for copy in sends:
        copy.wait_recv()
    for t in range(2):
        base[:, :, 256 * t : 256 * t + 256] = (sent[t, 0] + got_in[t, 1]) + (got_in[t, 2] + got_in[t, 3])
    copies.append(pltpu.make_async_copy(base, base_out, out_sem.at[1]))
    copies[2].start()
    for copy in sends:
        copy.wait_send()
    for copy in lows:
        copy.wait()
    for copy in copies:
        copy.wait()


def finish(base, low, late, q1, q2, q3, l1, l2, l3, e0, tall, out):
    for i, t in ((0, 0), (1, 3)):
        out[:, :, 256 * t : 256 * t + 256] = late[i] + (l2[i].astype(F32) + (l1[i].astype(F32) + l3[i].astype(F32)))
    total = low[...] + (q2[...].astype(F32) + (q1[...].astype(F32) + q3[...].astype(F32)))
    hi, lo = halves(total)
    hi, lo = halves(dot(tall[...], jnp.concatenate([hi, lo], axis=0)))
    for t in (0, 1):
        cols = slice(128 * t, 128 * t + 256)
        got = dot(jnp.concatenate([hi[:, cols], lo[:, cols]], axis=0), e0[...])
        cols = slice(256 * t, 256 * t + 256)
        out[:, :, 256 + 256 * t : 512 + 256 * t] = base[:, :, cols].astype(F32) + (got[0:96] + got[96:192]).reshape(3, 32, 256)


def solution(mesh):
    n_strip, n_lvl = mesh.shape["strip"], mesh.shape["lvl"]
    table = constants()

    def per_device(photos, seams, offsets):
        far = pl.BlockSpec(memory_space=pltpu.HBM)
        given = [jnp.asarray(table[name]) for name in NAMES]
        dma = pltpu.SemaphoreType.DMA
        tile = (4, 3, 32, 256)
        strip = (3, 32, N)
        low_shape = jax.ShapeDtypeStruct((64, 384), BF)
        late_shape = jax.ShapeDtypeStruct((2, 3, 32, 256), BF)
        results = pl.pallas_call(
            functools.partial(kernel, n_strip, n_lvl),
            out_shape=(
                jax.ShapeDtypeStruct((3, 32, 512), BF),
                jax.ShapeDtypeStruct((64, 384), F32),
                jax.ShapeDtypeStruct((2, 3, 32, 256), F32),
                *[low_shape] * 3,
                *[late_shape] * 3,
            ),
            in_specs=[far] * (3 + len(NAMES)),
            out_specs=(far,) * 9,
            scratch_shapes=[
                *[pltpu.VMEM(a.shape[1:] if name == "h35" else a.shape, a.dtype) for name, a in zip(NAMES, given)],
                dma((len(NAMES) + 5,)),
                pltpu.VMEM((4, 3, 64, N), BF),
                pltpu.SMEM((4,), jnp.int32),
                pltpu.VMEM((4, 2, 64), jnp.int32),
                pltpu.VMEM((256, 128), F32),
                pltpu.VMEM((256, 128), F32),
                pltpu.VMEM((4, 128, 1280), BF),
                pltpu.VMEM((512, 640), BF),
                pltpu.VMEM((512, 640), BF),
                pltpu.VMEM((512, 384), BF),
                pltpu.VMEM((256, 1280), BF),
                pltpu.VMEM((4, 384, 256), BF),
                pltpu.VMEM((4, 384, 256), BF),
                pltpu.VMEM((2, *tile), BF),
                pltpu.VMEM((2, *tile), BF),
                pltpu.VMEM((3, 32, 512), BF),
                pltpu.VMEM((3, 64, 384), BF),
                pltpu.VMEM((64, 384), F32),
                pltpu.VMEM((4, 3, 256, 256), BF),
                pltpu.VMEM((2, 3, 3, 32, 256), BF),
                pltpu.VMEM((2, 3, 32, 256), F32),
                dma((3,)),
                *[dma((2,))] * 2,
                dma((2, 3)), dma((2, 3)), dma((3,)), dma((3,)), dma((2, 3)), dma((2, 3)),
            ],
            compiler_params=pltpu.CompilerParams(collective_id=0, has_side_effects=True),
        )(offsets, photos, seams, *given)
        near = pl.BlockSpec(memory_space=pltpu.VMEM)
        return pl.pallas_call(
            finish, out_shape=jax.ShapeDtypeStruct(strip, F32), in_specs=[near] * 11, out_specs=near
        )(*results, jnp.asarray(table["e0"]), jnp.asarray(table["tall"]))

    placed = (P("strip", None, None, "lvl"), P("strip", None, None), P("strip"))
    return jax.shard_map(
        per_device, mesh=mesh, in_specs=placed, out_specs=P(None, "strip", "lvl"), check_vma=False
    )
```
